256 devices in a mesh: noise: 8 (over z), dp: 32 (over x, y, core).
Axes of the slice: x: 4, y: 4, z: 8, core: 2. Of those that a mesh axis runs over, the one named last changes fastest.
Arguments:
- noise_points: float32 [12288, 512], P('noise'), may hold values from -1.5 to 1.5
- data_points: float32 [12288, 512], P('dp', 'noise'), may hold values from -1.5 to 1.5
- noise_blocks: int32 [8], P('noise'), may hold values from 1 to 12, as said below
- data_blocks: int32 [32], P('dp'), may hold values from 1 to 3, as said below
Outputs:
- noise_potential: float32 [12288], P('noise')
- data_potential: float32 [12288], P('dp')
- noise_target: float32 [512, 12288], P('dp', 'noise')
- data_target: float32 [512, 12288], P('noise', 'dp')
The draws below stay inside these ranges and needn't reach their ends.
Inputs may be any that keep to these rules, and one draw needn't show every extreme that they name: `noise_blocks`: blocks 0 up to this count of each device's 12 slots are live, the rest padding; some device has all 12 live. `data_blocks`: blocks 0 up to this count of each device's 3 slots are live, the rest padding; some device has all 3 live.
All inputs are finite; a program needn't handle non-finite values.
Results may differ from the reference program's by a relative error of at most 0.0003.
Values sent between devices are 32-bit elements; how exact they have to be, the bound alone decides.
No kernel may reach another device: no remote copies, remote signals or barrier semaphores. Data moves between devices by JAX's collectives and lax.ppermute only.
A program may use at most 64 MiB of HBM per device.

```python
import jax
import jax.numpy as jnp
from jax import lax

P_SIZE = 512
BLOCK = 128
XB_DEV = 12
YB_DEV = 3
ITERS = 3
NX = 12288
NY = 12288


def point_pair(key):
    base = jax.random.fold_in(key, 4242)
    key_noise, key_data = jax.random.split(base, 2)
    rows_dev = XB_DEV * BLOCK
    cols_dev = YB_DEV * BLOCK
    groups = NX // rows_dev
    data_groups = NY // cols_dev
    noise = jax.random.normal(key_noise, (NX, P_SIZE), jnp.float32) * 0.125
    data = jax.random.normal(key_data, (NY, P_SIZE), jnp.float32) * 0.125
    far_rows = jnp.arange(groups, dtype=jnp.int32) * rows_dev + 2
    far_cols = jnp.arange(data_groups, dtype=jnp.int32) * cols_dev + 2
    row_strength = 14.0 + 7.0 * (jnp.arange(groups, dtype=jnp.int32) % 3).astype(jnp.float32)
    col_strength = 14.0 + 7.0 * (jnp.arange(data_groups, dtype=jnp.int32) % 3).astype(jnp.float32)
    noise = noise.at[far_rows].add(jnp.sqrt(row_strength / P_SIZE)[:, None])
    data = data.at[far_cols].add(-jnp.sqrt(col_strength / P_SIZE)[:, None])
    return (jnp.clip(noise, -1.5, 1.5), jnp.clip(data, -1.5, 1.5))


def draw_noise_points(key, part):
    return point_pair(key)[0]


def draw_data_points(key, part):
    return point_pair(key)[1]


def block_counts(key, count, most):
    key_base, key_full = jax.random.split(key, 2)
    counts = jax.random.randint(key_base, (count,), 1, most // 2 + 1, jnp.int32)
    full = jax.random.randint(key_full, (), 0, count, jnp.int32)
    return counts.at[full].set(most)


def draw_noise_blocks(key, part):
    return block_counts(jax.random.fold_in(key, 11), NX // (XB_DEV * BLOCK), XB_DEV)


def draw_data_blocks(key, part):
    return block_counts(jax.random.fold_in(key, 13), NY // (YB_DEV * BLOCK), YB_DEV)


def setup_inputs(seed: int = 0) -> dict:
    key_of = jax.random.split(jax.random.key(seed), 5)
    noise_points = draw_noise_points(jax.random.fold_in(key_of[4], 71), 0)
    data_points = draw_data_points(jax.random.fold_in(key_of[4], 71), 0)
    noise_blocks = draw_noise_blocks(jax.random.fold_in(key_of[4], 71), 0)
    data_blocks = draw_data_blocks(jax.random.fold_in(key_of[4], 71), 0)
    return {"noise_points": noise_points, "data_points": data_points, "noise_blocks": noise_blocks, "data_blocks": data_blocks}


SMOOTHING_TEMP = 0.125


def pair_cost(rows, cols, col_sq):
    row_sq = jnp.sum(rows * rows, axis=1)
    cross = jnp.dot(rows, cols.T, precision=lax.Precision.HIGHEST, preferred_element_type=jnp.float32)
    return row_sq[:, None] + col_sq[None, :] - 2.0 * cross


def reference(noise_points, data_points, noise_blocks, data_blocks):
    rows_dev = XB_DEV * BLOCK
    cols_dev = YB_DEV * BLOCK
    groups = NX // rows_dev
    log_noise_mass = -jnp.log((jnp.sum(noise_blocks) * BLOCK).astype(jnp.float32))
    log_data_mass = -jnp.log((jnp.sum(data_blocks) * BLOCK).astype(jnp.float32))
    row_limit = jnp.repeat((noise_blocks * BLOCK).astype(jnp.int32), rows_dev, total_repeat_length=NX)
    col_limit = jnp.repeat((data_blocks * BLOCK).astype(jnp.int32), cols_dev, total_repeat_length=NY)
    row_active = (jnp.arange(NX, dtype=jnp.int32) % rows_dev) < row_limit
    column_active = (jnp.arange(NY, dtype=jnp.int32) % cols_dev) < col_limit
    grouped = noise_points.reshape(groups, rows_dev, P_SIZE)
    live_grouped = row_active.reshape(groups, rows_dev)
    col_sq = jnp.sum(data_points * data_points, axis=1)

    def row_scores(points, data_potential):
        transport_cost = pair_cost(points, data_points, col_sq)
        return jnp.where(column_active[None, :], (data_potential[None, :] - transport_cost) / SMOOTHING_TEMP + log_data_mass, -jnp.inf)

    def row_threshold(data_potential):
        def one(points):
            pair_scores = row_scores(points, data_potential)
            peak = jnp.max(pair_scores, axis=1)
            return peak + jnp.log(jnp.sum(jnp.exp(pair_scores - peak[:, None]), axis=1))
        return lax.map(one, grouped).reshape(NX)

    def column_level(noise_potential):
        duals = noise_potential.reshape(groups, rows_dev)

        def step(carry, items):
            peak, mass = carry
            points, active_pairs, dual_value = items
            transport_cost = pair_cost(points, data_points, col_sq)
            pair_scores = jnp.where(active_pairs[:, None], (dual_value[:, None] - transport_cost) / SMOOTHING_TEMP + log_noise_mass, -jnp.inf)
            top = jnp.maximum(peak, jnp.max(pair_scores, axis=0))
            mass = mass * jnp.exp(peak - top) + jnp.sum(jnp.exp(pair_scores - top[None, :]), axis=0)
            return (top, mass), None

        init = (jnp.full((NY,), -jnp.inf, jnp.float32), jnp.zeros((NY,), jnp.float32))
        (peak, mass), _ = lax.scan(step, init, (grouped, live_grouped, duals))
        return peak + jnp.log(mass)

    data_potential = jnp.zeros((NY,), jnp.float32)
    noise_potential = jnp.zeros((NX,), jnp.float32)
    for turn in range(ITERS):
        noise_potential = jnp.where(row_active, -SMOOTHING_TEMP * row_threshold(data_potential), 0.0)
        data_potential = jnp.where(column_active, -SMOOTHING_TEMP * column_level(noise_potential), 0.0)

    def project_rows(items):
        points, active_pairs = items
        pair_scores = row_scores(points, data_potential)
        peak = jnp.max(pair_scores, axis=1)
        level = peak + jnp.log(jnp.sum(jnp.exp(pair_scores - peak[:, None]), axis=1))
        plan_weights = jnp.where(active_pairs[:, None] & column_active[None, :], jnp.exp(pair_scores - level[:, None]), 0.0)
        return jnp.dot(plan_weights, data_points, precision=lax.Precision.HIGHEST, preferred_element_type=jnp.float32)

    noise_target = lax.map(project_rows, (grouped, live_grouped)).reshape(NX, P_SIZE).T

    duals = noise_potential.reshape(groups, rows_dev)

    def project_cols(total, items):
        points, active_pairs, dual_value = items
        transport_cost = pair_cost(points, data_points, col_sq)
        plan_weights = jnp.where(active_pairs[:, None] & column_active[None, :], jnp.exp((dual_value[:, None] + data_potential[None, :] - transport_cost) / SMOOTHING_TEMP + log_noise_mass), 0.0)
        total = total + jnp.dot(plan_weights.T, points, precision=lax.Precision.HIGHEST, preferred_element_type=jnp.float32)
        return total, None

    summed, _ = lax.scan(project_cols, jnp.zeros((NY, P_SIZE), jnp.float32), (grouped, live_grouped, duals))
    return noise_potential, data_potential, noise_target, summed.T
```

```python
import jax
import jax.numpy as jnp
from jax import lax
from jax.experimental import pallas as pl
from jax.experimental.pallas import tpu as pltpu
from jax.sharding import Mesh, PartitionSpec as P


BLOCK = 128
ITERS = 3
SMOOTHING_TEMP = 0.125
SHARP = 1.0 / SMOOTHING_TEMP

F32 = jnp.float32
BF16 = jnp.bfloat16
NZ, NXY, NC = 8, 16, 2
ROWS, COLS, DIM = 1536, 384, 512
RB, CB = ROWS // BLOCK, COLS // BLOCK
CHUNK = DIM // NZ
OWN = DIM // (NXY * NC)
LROWS = 16
TOPS = RB * OWN
LEVELS = TOPS + RB
PIECE = TOPS + 2 * RB

SMEM = pl.BlockSpec(memory_space=pltpu.SMEM)
VMEM = pl.BlockSpec(memory_space=pltpu.VMEM)


def shaped(shape, dtype=F32):
    return jax.ShapeDtypeStruct(shape, dtype)


def call(body, outs, ins, scratch=(), limit=16):
    return pl.pallas_call(
        body,
        out_shape=outs,
        in_specs=ins,
        out_specs=jax.tree.map(lambda _: VMEM, outs),
        scratch_shapes=scratch,
        cost_estimate=pl.CostEstimate(flops=1000000, transcendentals=0, bytes_accessed=4000000),
        compiler_params=pltpu.CompilerParams(vmem_limit_bytes=limit << 20),
    )


def halves(value):
    high = value.astype(BF16)
    return high, (value - high.astype(F32)).astype(BF16)


def dot(a, b, dims):
    return lax.dot_general(a, b, (dims, ((), ())), preferred_element_type=F32)


def dot3(a, b, dims):
    return dot(a[0], b[0], dims) + (dot(a[0], b[1], dims) + dot(a[1], b[0], dims))


def diagonal():
    return lax.broadcasted_iota(jnp.int32, (BLOCK, BLOCK), 0) == lax.broadcasted_iota(
        jnp.int32, (BLOCK, BLOCK), 1
    )


def to_row(column, eye):
    return jnp.sum(jnp.where(eye, column, 0.0), axis=0, keepdims=True)


def to_column(row, eye):
    return jnp.sum(jnp.where(eye, jnp.broadcast_to(row, (BLOCK, BLOCK)), 0.0), axis=1, keepdims=True)


def prepare_body(points, high, low, turned_high, turned_low, squares):
    for k in range(0, ROWS, 256):
        part = points[k : k + 256, :]
        squares[k : k + 256, :] = jnp.sum(part * part, axis=1, keepdims=True)
        a, b = halves(part)
        high[k : k + 256, :] = a
        low[k : k + 256, :] = b
        a, b = halves(part.T)
        turned_high[:, k : k + 256] = a
        turned_low[:, k : k + 256] = b


def row_lse(cost, bias, k):
    scores = bias - cost[k * BLOCK : (k + 1) * BLOCK, :]
    top = jnp.max(scores, axis=1, keepdims=True)
    return top + jnp.log(jnp.sum(jnp.exp(scores - top), axis=1, keepdims=True))


def live_columns(info):
    return lax.broadcasted_iota(jnp.int32, (1, COLS), 1) < info[3] * BLOCK


def store_count(out, row, count):
    out[row : row + 1, :] = jnp.full((1, BLOCK), (count * BLOCK).astype(F32))


def cost_body(info, high, low, squares, *refs):
    pieces, (cost, out, turned, data_high, data_low) = refs[:NZ], refs[NZ:]
    square = jnp.zeros((1, COLS), F32)
    for s in range(NZ):
        z = lax.rem(info[0] + (NZ - s), NZ)
        piece = pieces[s][...]
        square += jnp.sum(piece * piece, axis=0, keepdims=True)
        a, b = halves(piece)
        at = pl.multiple_of(z * CHUNK, CHUNK)
        data_high[pl.ds(at, CHUNK), :] = a
        data_low[pl.ds(at, CHUNK), :] = b
        for q in range(CHUNK // OWN):
            to = pl.multiple_of((z * 2 + q // 2) * OWN, OWN)
            turned[q % 2, 0, pl.ds(to, OWN), :] = a[q * OWN : (q + 1) * OWN]
            turned[q % 2, 1, pl.ds(to, OWN), :] = b[q * OWN : (q + 1) * OWN]
    eye = diagonal()
    bias = jnp.where(live_columns(info), 0.0, -jnp.inf)
    both = (data_high[...], data_low[...])
    for k in range(0, ROWS, 256):
        cross = dot3((high[k : k + 256, :], low[k : k + 256, :]), both, ((1,), (0,)))
        cost[k : k + 256, :] = SHARP * (squares[k : k + 256, :] + square - 2.0 * cross)
    out[...] = jnp.zeros((LROWS, BLOCK), F32)
    for k in range(RB):
        out[k : k + 1, :] = to_row(row_lse(cost, bias, k), eye)
    store_count(out, RB, info[3])


def joined(values):
    top = jnp.max(values, axis=0)
    return top + jnp.log(jnp.sum(jnp.exp(values - top[None]), axis=0))


def column_bias(got, info):
    values = got[...]
    total = jnp.sum(values[:, CB, :], axis=0, keepdims=True)
    level = joined(values)
    parts = [-(level[k : k + 1, :] - jnp.log(total)) for k in range(CB)]
    return jnp.where(live_columns(info), jnp.concatenate(parts, axis=1), -jnp.inf)


def row_body(info, got, cost, out):
    bias = column_bias(got, info)
    eye = diagonal()
    out[...] = jnp.zeros((LROWS, BLOCK), F32)
    for k in range(RB):
        out[k : k + 1, :] = to_row(row_lse(cost, bias, k), eye)
    store_count(out, RB, info[3])


def column_body(info, got, cost, out, dual, column):
    values = got[...]
    total = jnp.sum(values[:, RB, :], axis=0, keepdims=True)
    duals = -(joined(values) - jnp.log(total))
    dual[...] = duals
    eye = diagonal()
    tops = []
    for k in range(RB):
        row = jnp.where(k < info[2], duals[k : k + 1, :], -jnp.inf)
        bias = to_column(row, eye)
        column[k * BLOCK : (k + 1) * BLOCK, :] = bias
        scores = bias - cost[k * BLOCK : (k + 1) * BLOCK, :]
        tops.append(jnp.max(scores.reshape(BLOCK // 8, 8, COLS), axis=0))
    top = tops[0]
    for k in range(1, RB):
        top = jnp.maximum(top, tops[k])
    top = jnp.max(top, axis=0, keepdims=True)
    mass = jnp.zeros((8, COLS), F32)
    for k in range(RB):
        part = slice(k * BLOCK, (k + 1) * BLOCK)
        scores = jnp.exp(column[part, :] - cost[part, :] - top)
        mass += jnp.sum(scores.reshape(BLOCK // 8, 8, COLS), axis=0)
    level = top + jnp.log(jnp.sum(mass, axis=0, keepdims=True))
    value = jnp.concatenate(
        [level[:, k * BLOCK : (k + 1) * BLOCK] for k in range(CB)]
        + [jnp.full((1, BLOCK), (info[2] * BLOCK).astype(F32))]
        + [jnp.zeros((8 - CB - 1, BLOCK), F32)],
        axis=0,
    )
    for z in range(NZ):
        out[z] = value


def project_noise_body(own, column, cost, turned_high, turned_low, out, weights_high, weights_low):
    level = jnp.concatenate([own[0, k : k + 1, :] for k in range(CB)], axis=1)
    for k in range(0, ROWS, 256):
        part = slice(k, k + 256)
        a, b = halves(jnp.exp(column[part, :] - cost[part, :] - level))
        weights_high[part, :] = a
        weights_low[part, :] = b
    both = (weights_high[...], weights_low[...])
    for k in range(0, DIM, 256):
        some = dot3((turned_high[k : k + 256, :], turned_low[k : k + 256, :]), both, ((1,), (0,)))
        for q in range(256 // CHUNK):
            for c in range(CB):
                out[k // CHUNK + q, c * CHUNK : (c + 1) * CHUNK, :] = some[
                    q * CHUNK : (q + 1) * CHUNK, c * BLOCK : (c + 1) * BLOCK
                ]


def spread(out, some, k):
    for p in range(NXY):
        for h in range(2):
            out[p, (k * 2 + h) * OWN : (k * 2 + h + 1) * OWN, :] = some[
                p * OWN : (p + 1) * OWN, h * BLOCK : (h + 1) * BLOCK
            ]


def project_data_body(info, got, cost, turned, out, high, low, dual, tops):
    bias = column_bias(got, info)
    dual[...] = bias
    eye = diagonal()
    for k in range(RB):
        part = slice(k * BLOCK, (k + 1) * BLOCK)
        scores = bias - cost[part, :]
        top = jnp.max(scores, axis=1, keepdims=True)
        weights = jnp.exp(scores - top)
        level = top + jnp.log(jnp.sum(weights, axis=1, keepdims=True))
        tops[k : k + 1, :] = to_row(top, eye)
        tops[RB + k : RB + k + 1, :] = to_row(level, eye)
        a, b = halves(weights)
        high[part, :] = a
        low[part, :] = b
    other = 1 - info[1]
    for k in range(ROWS // 256):
        part = slice(k * 256, (k + 1) * 256)
        some = dot3((turned[other, 0], turned[other, 1]), (high[part, :], low[part, :]), ((1,), (1,)))
        spread(out, some, k)
    for p in range(NXY):
        out[p, TOPS:PIECE, :] = tops[...]


def project_own_body(info, turned, high, low, out):
    mine = info[1]
    for k in range(ROWS // 256):
        part = slice(k * 256, (k + 1) * 256)
        some = dot3((turned[mine, 0], turned[mine, 1]), (high[part, :], low[part, :]), ((1,), (1,)))
        spread(out, some, k)


def merge_body(own, own_tops, came, out):
    a, b = own_tops[RB : 2 * RB, :], came[0, LEVELS:PIECE, :]
    top = jnp.maximum(a, b)
    level = top + jnp.log(jnp.exp(a - top) + jnp.exp(b - top))
    a, b = jnp.exp(own_tops[0:RB, :] - level), jnp.exp(came[0, TOPS:LEVELS, :] - level)
    for k in range(RB):
        part = slice(k * OWN, (k + 1) * OWN)
        out[:, part, :] = (
            own[:, part, :] * a[k : k + 1, :][None] + came[:, part, :] * b[k : k + 1, :][None]
        )
    for p in range(NXY):
        out[p, LEVELS:PIECE, :] = level
        out[p, TOPS:LEVELS, :] = level


def finish_noise_body(info, came, out):
    levels = came[:, LEVELS:PIECE, :]
    shares = jnp.exp(levels - joined(levels)[None])
    for k in range(RB):
        part = slice(k * OWN, (k + 1) * OWN)
        total = jnp.sum(came[:, part, :] * shares[:, k : k + 1, :], axis=0)
        out[:, k * BLOCK : (k + 1) * BLOCK] = jnp.where(k < info[2], total, 0.0)


def finish_data_body(info, came, got, out):
    levels = got[...]
    shares = jnp.exp(levels - joined(levels)[None])
    for k in range(CB):
        part = slice(k * CHUNK, (k + 1) * CHUNK)
        total = jnp.sum(came[:, part, :] * shares[:, k : k + 1, :], axis=0)
        out[:, k * BLOCK : (k + 1) * BLOCK] = jnp.where(k < info[3], total, 0.0)


CORES = [(0, 1), (1, 0)]


def over_dp(lse):
    came = lax.ppermute(lse, "c", CORES)
    top = jnp.maximum(lse, came)
    both = top + jnp.log(jnp.exp(lse - top) + jnp.exp(came - top))
    counts = lax.broadcasted_iota(jnp.int32, (LROWS, BLOCK), 0) == RB
    both = jnp.where(counts, lse + came, both)
    return lax.all_to_all(
        jnp.broadcast_to(both[None], (NXY, LROWS, BLOCK)), ("x", "y"), 0, 0, tiled=True
    )


def over_noise(pieces):
    return lax.all_to_all(pieces, "z", 0, 0, tiled=True)


def on_device(noise_points, data_points, noise_blocks, data_blocks):
    info = jnp.concatenate(
        [lax.axis_index("z").reshape(1), lax.axis_index("c").reshape(1), noise_blocks, data_blocks]
    )
    mine = data_points.T
    pieces = [mine] + [
        lax.ppermute(mine, "z", [(i, (i + s) % NZ) for i in range(NZ)]) for s in range(1, NZ)
    ]
    high, low, turned_high, turned_low, squares = call(
        prepare_body,
        (
            shaped((ROWS, DIM), BF16),
            shaped((ROWS, DIM), BF16),
            shaped((DIM, ROWS), BF16),
            shaped((DIM, ROWS), BF16),
            shaped((ROWS, 1)),
        ),
        [VMEM],
    )(noise_points)
    cost, lse, turned = call(
        cost_body,
        (shaped((ROWS, COLS)), shaped((LROWS, BLOCK)), shaped((NC, 2, DIM // NC, COLS), BF16)),
        [SMEM] + [VMEM] * (3 + NZ),
        [pltpu.VMEM((DIM, COLS), BF16), pltpu.VMEM((DIM, COLS), BF16)],
    )(info, high, low, squares, *pieces)
    for turn in range(ITERS):
        if turn:
            lse = call(row_body, shaped((LROWS, BLOCK)), [SMEM, VMEM, VMEM])(info, got, cost)
        rows = over_dp(lse)
        sent, dual, column = call(
            column_body,
            (shaped((NZ, 8, BLOCK)), shaped((LROWS, BLOCK)), shaped((ROWS, 1))),
            [SMEM, VMEM, VMEM],
        )(info, rows, cost)
        got = over_noise(sent)
    halfway = call(
        project_noise_body,
        shaped((NZ, CB * CHUNK, BLOCK)),
        [VMEM] * 5,
        [pltpu.VMEM((ROWS, COLS), BF16), pltpu.VMEM((ROWS, COLS), BF16)],
    )(sent, column, cost, turned_high, turned_low)
    got, halfway = lax.optimization_barrier((got, halfway))
    data_came = over_noise(halfway)
    theirs, weights_high, weights_low, data_dual, level = call(
        project_data_body,
        (
            shaped((NXY, PIECE, BLOCK)),
            shaped((ROWS, COLS), BF16),
            shaped((ROWS, COLS), BF16),
            shaped((1, COLS)),
            shaped((2 * RB, BLOCK)),
        ),
        [SMEM, VMEM, VMEM, VMEM],
    )(info, got, cost, turned)
    came = lax.ppermute(theirs, "c", CORES)
    own = call(
        project_own_body, shaped((NXY, RB * OWN, BLOCK)), [SMEM, VMEM, VMEM, VMEM]
    )(info, turned, weights_high, weights_low)
    merged = call(merge_body, shaped((NXY, PIECE, BLOCK)), [VMEM] * 3)(own, level, came)
    noise_came = lax.all_to_all(merged, ("x", "y"), 0, 0, tiled=True)
    noise_target = call(finish_noise_body, shaped((OWN, ROWS)), [SMEM, VMEM])(info, noise_came)
    data_target = call(
        finish_data_body, shaped((CHUNK, COLS)), [SMEM, VMEM, VMEM]
    )(info, data_came, got)
    row_live = jnp.arange(ROWS, dtype=jnp.int32) < noise_blocks[0] * BLOCK
    column_live = jnp.arange(COLS, dtype=jnp.int32) < data_blocks[0] * BLOCK
    noise_potential = jnp.where(row_live, SMOOTHING_TEMP * dual[:RB].reshape(ROWS), 0.0)
    data_potential = jnp.where(column_live, SMOOTHING_TEMP * data_dual.reshape(COLS), 0.0)
    return noise_potential, data_potential, noise_target, data_target


def solution(mesh):
    axes = Mesh(mesh.devices.reshape(NZ, 4, 4, NC), ("z", "x", "y", "c"))
    dp = ("x", "y", "c")
    return jax.shard_map(
        on_device,
        mesh=axes,
        in_specs=(P("z", None), P(dp, "z"), P("z"), P(dp)),
        out_specs=(P("z"), P(dp), P(dp, "z"), P("z", dp)),
        check_vma=False,
    )
```

```python
import jax
import jax.numpy as jnp
from jax import lax
from jax.experimental import pallas as pl
from jax.experimental.pallas import tpu as pltpu
from jax.sharding import Mesh, PartitionSpec as P


BLOCK = 128
ITERS = 3
SMOOTHING_TEMP = 0.125
SHARP = 1.0 / SMOOTHING_TEMP

F32 = jnp.float32
BF16 = jnp.bfloat16
NZ, NXY, NC = 8, 16, 2
ROWS, COLS, DIM = 1536, 384, 512
RB, CB = ROWS // BLOCK, COLS // BLOCK
CHUNK = DIM // NZ
OWN = DIM // (NXY * NC)
LROWS = 16
TOPS = RB * OWN
LEVELS = TOPS + RB
PIECE = TOPS + 2 * RB

SMEM = pl.BlockSpec(memory_space=pltpu.SMEM)
VMEM = pl.BlockSpec(memory_space=pltpu.VMEM)
HBM = pl.BlockSpec(memory_space=pltpu.HBM)


def shaped(shape, dtype=F32):
    return jax.ShapeDtypeStruct(shape, dtype)


def call(body, outs, ins, scratch=(), limit=16, places=None):
    return pl.pallas_call(
        body,
        out_shape=outs,
        in_specs=ins,
        out_specs=places or jax.tree.map(lambda _: VMEM, outs),
        scratch_shapes=scratch,
        cost_estimate=pl.CostEstimate(flops=1000000, transcendentals=0, bytes_accessed=4000000),
        compiler_params=pltpu.CompilerParams(vmem_limit_bytes=limit << 20),
    )


def halves(value):
    high = value.astype(BF16)
    return high, (value - high.astype(F32)).astype(BF16)


def dot(a, b, dims):
    return lax.dot_general(a, b, (dims, ((), ())), preferred_element_type=F32)


def dot3(a, b, dims):
    return dot(a[0], b[0], dims) + (dot(a[0], b[1], dims) + dot(a[1], b[0], dims))


def diagonal():
    return lax.broadcasted_iota(jnp.int32, (BLOCK, BLOCK), 0) == lax.broadcasted_iota(
        jnp.int32, (BLOCK, BLOCK), 1
    )


def to_row(column, eye):
    return jnp.sum(jnp.where(eye, column, 0.0), axis=0, keepdims=True)


def to_column(row, eye):
    return jnp.sum(jnp.where(eye, jnp.broadcast_to(row, (BLOCK, BLOCK)), 0.0), axis=1, keepdims=True)


def prepare_body(
    place, core, nblk, dblk, points, high, low, turned_high, turned_low, squares, th, tl, sems
):
    for k in range(0, ROWS, 256):
        part = points[k : k + 256, :]
        squares[k : k + 256, :] = jnp.sum(part * part, axis=1, keepdims=True)
        a, b = halves(part)
        high[k : k + 256, :] = a
        low[k : k + 256, :] = b
        a, b = halves(part.T)
        th[:, k : k + 256] = a
        tl[:, k : k + 256] = b
    copies = [
        pltpu.make_async_copy(th, turned_high, sems.at[0]),
        pltpu.make_async_copy(tl, turned_low, sems.at[1]),
    ]
    for copy in copies:
        copy.start()
    for copy in copies:
        copy.wait()


def row_lse(cost, bias, k):
    scores = bias - cost[k * BLOCK : (k + 1) * BLOCK, :]
    top = jnp.max(scores, axis=1, keepdims=True)
    return top + jnp.log(jnp.sum(jnp.exp(scores - top), axis=1, keepdims=True))


def live_columns(dblk):
    return lax.broadcasted_iota(jnp.int32, (1, COLS), 1) < dblk[0] * BLOCK


def store_count(out, row, count):
    out[row : row + 1, :] = jnp.full((1, BLOCK), (count * BLOCK).astype(F32))


def cost_body(place, core, nblk, dblk, high, low, squares, *refs):
    pieces, (cost, out, turned, data_high, data_low) = refs[:NZ], refs[NZ:]
    square = jnp.zeros((1, COLS), F32)
    for s in range(NZ):
        z = lax.rem(place[0] + (NZ - s), NZ)
        piece = pieces[s][...]
        square += jnp.sum(piece * piece, axis=0, keepdims=True)
        a, b = halves(piece)
        at = pl.multiple_of(z * CHUNK, CHUNK)
        data_high[pl.ds(at, CHUNK), :] = a
        data_low[pl.ds(at, CHUNK), :] = b
        for q in range(CHUNK // OWN):
            to = pl.multiple_of((z * 2 + q // 2) * OWN, OWN)
            turned[q % 2, 0, pl.ds(to, OWN), :] = a[q * OWN : (q + 1) * OWN]
            turned[q % 2, 1, pl.ds(to, OWN), :] = b[q * OWN : (q + 1) * OWN]
    eye = diagonal()
    bias = jnp.where(live_columns(dblk), 0.0, -jnp.inf)
    both = (data_high[...], data_low[...])
    for k in range(0, ROWS, 256):
        cross = dot3((high[k : k + 256, :], low[k : k + 256, :]), both, ((1,), (0,)))
        cost[k : k + 256, :] = SHARP * (squares[k : k + 256, :] + square - 2.0 * cross)
    out[...] = jnp.zeros((LROWS, BLOCK), F32)
    for k in range(RB):
        out[k : k + 1, :] = to_row(row_lse(cost, bias, k), eye)
    store_count(out, RB, dblk[0])


def joined(values):
    top = jnp.max(values, axis=0)
    return top + jnp.log(jnp.sum(jnp.exp(values - top[None]), axis=0))


def column_bias(got, dblk):
    values = got[...]
    total = jnp.sum(values[:, CB, :], axis=0, keepdims=True)
    level = joined(values)
    parts = [-(level[k : k + 1, :] - jnp.log(total)) for k in range(CB)]
    return jnp.where(live_columns(dblk), jnp.concatenate(parts, axis=1), -jnp.inf)


def row_body(dblk, got, cost, out):
    bias = column_bias(got, dblk)
    eye = diagonal()
    out[...] = jnp.zeros((LROWS, BLOCK), F32)
    for k in range(RB):
        out[k : k + 1, :] = to_row(row_lse(cost, bias, k), eye)
    store_count(out, RB, dblk[0])


def column_body(nblk, got, cost, out, dual, column):
    values = got[...]
    total = jnp.sum(values[:, RB, :], axis=0, keepdims=True)
    duals = -(joined(values) - jnp.log(total))
    dual[...] = duals
    eye = diagonal()
    tops = []
    for k in range(RB):
        row = jnp.where(k < nblk[0], duals[k : k + 1, :], -jnp.inf)
        bias = to_column(row, eye)
        column[k * BLOCK : (k + 1) * BLOCK, :] = bias
        scores = bias - cost[k * BLOCK : (k + 1) * BLOCK, :]
        tops.append(jnp.max(scores.reshape(BLOCK // 8, 8, COLS), axis=0))
    top = tops[0]
    for k in range(1, RB):
        top = jnp.maximum(top, tops[k])
    top = jnp.max(top, axis=0, keepdims=True)
    mass = jnp.zeros((8, COLS), F32)
    for k in range(RB):
        part = slice(k * BLOCK, (k + 1) * BLOCK)
        scores = jnp.exp(column[part, :] - cost[part, :] - top)
        mass += jnp.sum(scores.reshape(BLOCK // 8, 8, COLS), axis=0)
    level = top + jnp.log(jnp.sum(mass, axis=0, keepdims=True))
    value = jnp.concatenate(
        [level[:, k * BLOCK : (k + 1) * BLOCK] for k in range(CB)]
        + [jnp.full((1, BLOCK), (nblk[0] * BLOCK).astype(F32))]
        + [jnp.zeros((8 - CB - 1, BLOCK), F32)],
        axis=0,
    )
    for z in range(NZ):
        out[z] = value


def project_noise_body(place, nblk, own, dual, cost, turned_high, turned_low, *refs):
    outs, (whole, th, tl, weights_high, weights_low, sems) = refs[:NZ], refs[NZ:]
    copies = [
        pltpu.make_async_copy(turned_high, th, sems.at[0]),
        pltpu.make_async_copy(turned_low, tl, sems.at[1]),
    ]
    for copy in copies:
        copy.start()
    level = jnp.concatenate([own[0, k : k + 1, :] for k in range(CB)], axis=1)
    eye = diagonal()
    for k in range(RB):
        part = slice(k * BLOCK, (k + 1) * BLOCK)
        row = jnp.where(k < nblk[0], dual[k : k + 1, :], -jnp.inf)
        a, b = halves(jnp.exp(to_column(row, eye) - cost[part, :] - level))
        weights_high[part, :] = a
        weights_low[part, :] = b
    for copy in copies:
        copy.wait()
    both = (weights_high[...], weights_low[...])
    for k in range(0, DIM, 256):
        some = dot3((th[k : k + 256, :], tl[k : k + 256, :]), both, ((1,), (0,)))
        for q in range(256 // CHUNK):
            for c in range(CB):
                whole[k // CHUNK + q, c * CHUNK : (c + 1) * CHUNK, :] = some[
                    q * CHUNK : (q + 1) * CHUNK, c * BLOCK : (c + 1) * BLOCK
                ]
    moves = [
        pltpu.make_async_copy(whole.at[lax.rem(place[0] + s, NZ)], outs[s], sems.at[2 + s])
        for s in range(NZ)
    ]
    for move in moves:
        move.start()
    for move in moves:
        move.wait()


def spread(out, some, k):
    for p in range(NXY):
        for h in range(2):
            out[p, (k * 2 + h) * OWN : (k * 2 + h + 1) * OWN, :] = some[
                p * OWN : (p + 1) * OWN, h * BLOCK : (h + 1) * BLOCK
            ]


def project_data_body(core, dblk, got, cost, turned, out, high, low, dual, tops):
    bias = column_bias(got, dblk)
    dual[...] = bias
    eye = diagonal()
    for k in range(RB):
        part = slice(k * BLOCK, (k + 1) * BLOCK)
        scores = bias - cost[part, :]
        top = jnp.max(scores, axis=1, keepdims=True)
        weights = jnp.exp(scores - top)
        level = top + jnp.log(jnp.sum(weights, axis=1, keepdims=True))
        tops[k : k + 1, :] = to_row(top, eye)
        tops[RB + k : RB + k + 1, :] = to_row(level, eye)
        a, b = halves(weights)
        high[part, :] = a
        low[part, :] = b
    other = 1 - core[0]
    for k in range(ROWS // 256):
        part = slice(k * 256, (k + 1) * 256)
        some = dot3((turned[other, 0], turned[other, 1]), (high[part, :], low[part, :]), ((1,), (1,)))
        spread(out, some, k)
    for p in range(NXY):
        out[p, TOPS:PIECE, :] = tops[...]


def project_own_body(core, turned, high, low, out):
    mine = core[0]
    for k in range(ROWS // 256):
        part = slice(k * 256, (k + 1) * 256)
        some = dot3((turned[mine, 0], turned[mine, 1]), (high[part, :], low[part, :]), ((1,), (1,)))
        spread(out, some, k)


def merge_body(own, own_tops, came, out):
    a, b = own_tops[RB : 2 * RB, :], came[0, LEVELS:PIECE, :]
    top = jnp.maximum(a, b)
    level = top + jnp.log(jnp.exp(a - top) + jnp.exp(b - top))
    a, b = jnp.exp(own_tops[0:RB, :] - level), jnp.exp(came[0, TOPS:LEVELS, :] - level)
    for k in range(RB):
        part = slice(k * OWN, (k + 1) * OWN)
        out[:, part, :] = (
            own[:, part, :] * a[k : k + 1, :][None] + came[:, part, :] * b[k : k + 1, :][None]
        )
    for p in range(NXY):
        out[p, LEVELS:PIECE, :] = level
        out[p, TOPS:LEVELS, :] = level


def finish_noise_body(nblk, came, out):
    levels = came[:, LEVELS:PIECE, :]
    shares = jnp.exp(levels - joined(levels)[None])
    for k in range(RB):
        part = slice(k * OWN, (k + 1) * OWN)
        total = jnp.sum(came[:, part, :] * shares[:, k : k + 1, :], axis=0)
        out[:, k * BLOCK : (k + 1) * BLOCK] = jnp.where(k < nblk[0], total, 0.0)


def finish_data_body(place, dblk, got, *refs):
    came, out = refs[:NZ], refs[NZ]
    level = joined(got[...])
    shares = [jnp.exp(got[lax.rem(place[0] + (NZ - s), NZ)] - level) for s in range(NZ)]
    for k in range(CB):
        part = slice(k * CHUNK, (k + 1) * CHUNK)
        total = came[0][part, :] * shares[0][k : k + 1, :]
        for s in range(1, NZ):
            total += came[s][part, :] * shares[s][k : k + 1, :]
        out[:, k * BLOCK : (k + 1) * BLOCK] = jnp.where(k < dblk[0], total, 0.0)


CORES = [(0, 1), (1, 0)]


def over_dp(lse):
    came = lax.ppermute(lse, "c", CORES)
    top = jnp.maximum(lse, came)
    both = top + jnp.log(jnp.exp(lse - top) + jnp.exp(came - top))
    counts = lax.broadcasted_iota(jnp.int32, (LROWS, BLOCK), 0) == RB
    both = jnp.where(counts, lse + came, both)
    return lax.all_to_all(
        jnp.broadcast_to(both[None], (NXY, LROWS, BLOCK)), ("x", "y"), 0, 0, tiled=True
    )


def over_noise(pieces):
    return lax.all_to_all(pieces, "z", 0, 0, tiled=True)


def on_device(noise_points, data_points, noise_blocks, data_blocks):
    place = lax.axis_index("z").reshape(1)
    core = lax.axis_index("c").reshape(1)
    mine, place, core = lax.optimization_barrier((data_points.T, place, core))
    pieces = [mine] + [
        lax.ppermute(mine, "z", [(i, (i + s) % NZ) for i in range(NZ)]) for s in range(1, NZ)
    ]
    high, low, turned_high, turned_low, squares = call(
        prepare_body,
        (
            shaped((ROWS, DIM), BF16),
            shaped((ROWS, DIM), BF16),
            pltpu.HBM((DIM, ROWS), BF16),
            pltpu.HBM((DIM, ROWS), BF16),
            shaped((ROWS, 1)),
        ),
        [SMEM] * 4 + [VMEM],
        [
            pltpu.VMEM((DIM, ROWS), BF16),
            pltpu.VMEM((DIM, ROWS), BF16),
            pltpu.SemaphoreType.DMA((2,)),
        ],
        limit=8,
        places=(VMEM, VMEM, HBM, HBM, VMEM),
    )(place, core, noise_blocks, data_blocks, noise_points)
    cost, lse, turned = call(
        cost_body,
        (shaped((ROWS, COLS)), shaped((LROWS, BLOCK)), shaped((NC, 2, DIM // NC, COLS), BF16)),
        [SMEM] * 4 + [VMEM] * (3 + NZ),
        [pltpu.VMEM((DIM, COLS), BF16), pltpu.VMEM((DIM, COLS), BF16)],
        limit=6,
    )(place, core, noise_blocks, data_blocks, high, low, squares, *pieces)
    for turn in range(ITERS):
        if turn:
            lse = call(row_body, shaped((LROWS, BLOCK)), [SMEM, VMEM, VMEM])(data_blocks, got, cost)
        rows = over_dp(lse)
        sent, dual = call(
            column_body,
            (shaped((NZ, 8, BLOCK)), shaped((LROWS, BLOCK))),
            [SMEM, VMEM, VMEM],
            [pltpu.VMEM((ROWS, 1), F32)],
        )(noise_blocks, rows, cost)
        got = over_noise(sent)
    halfway = call(
        project_noise_body,
        [pltpu.HBM((CB * CHUNK, BLOCK), F32) for _ in range(NZ)],
        [SMEM, SMEM, VMEM, VMEM, VMEM, HBM, HBM],
        [
            pltpu.VMEM((NZ, CB * CHUNK, BLOCK), F32),
            pltpu.VMEM((DIM, ROWS), BF16),
            pltpu.VMEM((DIM, ROWS), BF16),
            pltpu.VMEM((ROWS, COLS), BF16),
            pltpu.VMEM((ROWS, COLS), BF16),
            pltpu.SemaphoreType.DMA((2 + NZ,)),
        ],
        places=[HBM] * NZ,
    )(
        place,
        noise_blocks,
        sent,
        dual,
        cost,
        pltpu.with_memory_space_constraint(turned_high, pltpu.HBM),
        pltpu.with_memory_space_constraint(turned_low, pltpu.HBM),
    )
    got, halfway = lax.optimization_barrier((got, halfway))
    data_came = [halfway[0]] + [
        lax.ppermute(halfway[s], "z", [(i, (i + s) % NZ) for i in range(NZ)])
        for s in range(1, NZ)
    ]
    theirs, weights_high, weights_low, data_dual, level = call(
        project_data_body,
        (
            shaped((NXY, PIECE, BLOCK)),
            shaped((ROWS, COLS), BF16),
            shaped((ROWS, COLS), BF16),
            shaped((1, COLS)),
            shaped((2 * RB, BLOCK)),
        ),
        [SMEM, SMEM, VMEM, VMEM, VMEM],
    )(core, data_blocks, got, cost, turned)
    came = lax.ppermute(theirs, "c", CORES)
    own = call(
        project_own_body, shaped((NXY, RB * OWN, BLOCK)), [SMEM, VMEM, VMEM, VMEM]
    )(core, turned, weights_high, weights_low)
    merged = call(merge_body, shaped((NXY, PIECE, BLOCK)), [VMEM] * 3)(own, level, came)
    noise_came = lax.all_to_all(merged, ("x", "y"), 0, 0, tiled=True)
    noise_target = call(finish_noise_body, shaped((OWN, ROWS)), [SMEM, VMEM])(
        noise_blocks, noise_came
    )
    data_target = call(
        finish_data_body, shaped((CHUNK, COLS)), [SMEM, SMEM] + [VMEM] * (1 + NZ)
    )(place, data_blocks, got, *data_came)
    row_live = jnp.arange(ROWS, dtype=jnp.int32) < noise_blocks[0] * BLOCK
    column_live = jnp.arange(COLS, dtype=jnp.int32) < data_blocks[0] * BLOCK
    noise_potential = jnp.where(row_live, SMOOTHING_TEMP * dual[:RB].reshape(ROWS), 0.0)
    data_potential = jnp.where(column_live, SMOOTHING_TEMP * data_dual.reshape(COLS), 0.0)
    return noise_potential, data_potential, noise_target, data_target


def solution(mesh):
    axes = Mesh(mesh.devices.reshape(NZ, 4, 4, NC), ("z", "x", "y", "c"))
    dp = ("x", "y", "c")
    return jax.shard_map(
        on_device,
        mesh=axes,
        in_specs=(P("z", None), P(dp, "z"), P("z"), P(dp)),
        out_specs=(P("z"), P(dp), P(dp, "z"), P("z", dp)),
        check_vma=False,
    )
```

```python
import jax
import jax.numpy as jnp
from jax import lax
from jax.experimental import pallas as pl
from jax.experimental.pallas import tpu as pltpu
from jax.sharding import Mesh, PartitionSpec as P


BLOCK = 128
ITERS = 3
SMOOTHING_TEMP = 0.125
SHARP = 1.0 / SMOOTHING_TEMP

F32 = jnp.float32
BF16 = jnp.bfloat16
NZ, NXY, NC = 8, 16, 2
ROWS, COLS, DIM = 1536, 384, 512
RB, CB = ROWS // BLOCK, COLS // BLOCK
CHUNK = DIM // NZ
OWN = DIM // (NXY * NC)
LROWS = 16
TOPS = RB * OWN
LEVELS = TOPS + RB
PIECE = TOPS + 2 * RB

SMEM = pl.BlockSpec(memory_space=pltpu.SMEM)
VMEM = pl.BlockSpec(memory_space=pltpu.VMEM)
HBM = pl.BlockSpec(memory_space=pltpu.HBM)


def shaped(shape, dtype=F32):
    return jax.ShapeDtypeStruct(shape, dtype)


def call(body, outs, ins, scratch=(), limit=16, places=None):
    return pl.pallas_call(
        body,
        out_shape=outs,
        in_specs=ins,
        out_specs=places or jax.tree.map(lambda _: VMEM, outs),
        scratch_shapes=scratch,
        cost_estimate=pl.CostEstimate(flops=1000000, transcendentals=0, bytes_accessed=4000000),
        compiler_params=pltpu.CompilerParams(vmem_limit_bytes=limit << 20),
    )


def halves(value):
    high = value.astype(BF16)
    return high, (value - high.astype(F32)).astype(BF16)


def dot(a, b, dims):
    return lax.dot_general(a, b, (dims, ((), ())), preferred_element_type=F32)


def dot3(a, b, dims):
    return dot(a[0], b[0], dims) + (dot(a[0], b[1], dims) + dot(a[1], b[0], dims))


def diagonal():
    return lax.broadcasted_iota(jnp.int32, (BLOCK, BLOCK), 0) == lax.broadcasted_iota(
        jnp.int32, (BLOCK, BLOCK), 1
    )


def to_row(column, eye):
    return jnp.sum(jnp.where(eye, column, 0.0), axis=0, keepdims=True)


def to_column(row, eye):
    return jnp.sum(jnp.where(eye, jnp.broadcast_to(row, (BLOCK, BLOCK)), 0.0), axis=1, keepdims=True)


def prepare_body(
    place, core, nblk, dblk, points, high, low, turned_high, turned_low, squares, th, tl, sems
):
    for k in range(0, ROWS, 256):
        part = points[k : k + 256, :]
        squares[k : k + 256, :] = jnp.sum(part * part, axis=1, keepdims=True)
        a, b = halves(part)
        for p in range(2):
            for q in range(NZ // 2):
                take = slice((2 * q + p) * CHUNK, (2 * q + p + 1) * CHUNK)
                high[p, k : k + 256, q * CHUNK : (q + 1) * CHUNK] = a[:, take]
                low[p, k : k + 256, q * CHUNK : (q + 1) * CHUNK] = b[:, take]
        a, b = halves(part.T)
        th[:, k : k + 256] = a
        tl[:, k : k + 256] = b
    copies = [
        pltpu.make_async_copy(th, turned_high, sems.at[0]),
        pltpu.make_async_copy(tl, turned_low, sems.at[1]),
    ]
    for copy in copies:
        copy.start()
    for copy in copies:
        copy.wait()


def row_lse(cost, bias, k):
    scores = bias - cost[k * BLOCK : (k + 1) * BLOCK, :]
    top = jnp.max(scores, axis=1, keepdims=True)
    return top + jnp.log(jnp.sum(jnp.exp(scores - top), axis=1, keepdims=True))


def live_columns(dblk):
    return lax.broadcasted_iota(jnp.int32, (1, COLS), 1) < dblk[0] * BLOCK


def store_count(out, row, count):
    out[row : row + 1, :] = jnp.full((1, BLOCK), (count * BLOCK).astype(F32))


def neighbour(z):
    return z + 1 - 2 * lax.rem(z, 2)


def chunk_of(z, q):
    return lax.rem(z + (NZ - 2 * q), NZ)


def half_product(z, four, high, low, data_high, data_low):
    square = jnp.zeros((1, COLS), F32)
    for q in range(NZ // 2):
        piece = four[q * CHUNK : (q + 1) * CHUNK, :]
        square += jnp.sum(piece * piece, axis=0, keepdims=True)
        a, b = halves(piece)
        at = pl.multiple_of(lax.div(chunk_of(z, q), 2) * CHUNK, CHUNK)
        data_high[pl.ds(at, CHUNK), :] = a
        data_low[pl.ds(at, CHUNK), :] = b
    both = (data_high[...], data_low[...])
    side = lax.rem(z, 2)

    def cross(k):
        part = slice(k, k + 256)
        return square - 2.0 * dot3((high[side, part, :], low[side, part, :]), both, ((1,), (0,)))

    return cross


def near_body(place, high, low, squares, four, cost, data_high, data_low):
    cross = half_product(place[0], four, high, low, data_high, data_low)
    for k in range(0, ROWS, 256):
        cost[k : k + 256, :] = squares[k : k + 256, :] + cross(k)


def cost_body(place, dblk, high, low, four, other, near, cost, out, turned, data_high, data_low):
    z = place[0]
    cross = half_product(neighbour(z), other, high, low, data_high, data_low)
    eye = diagonal()
    bias = jnp.where(live_columns(dblk), 0.0, -jnp.inf)
    out[...] = jnp.zeros((LROWS, BLOCK), F32)
    for k in range(0, ROWS, 256):
        cost[k : k + 256, :] = SHARP * (near[k : k + 256, :] + cross(k))
    for k in range(RB):
        out[k : k + 1, :] = to_row(row_lse(cost, bias, k), eye)
    store_count(out, RB, dblk[0])
    for source, came in ((z, four), (neighbour(z), other)):
        for q in range(NZ // 2):
            for h in range(CHUNK // OWN):
                a, b = halves(came[q * CHUNK + h * OWN : q * CHUNK + (h + 1) * OWN, :])
                to = pl.multiple_of((chunk_of(source, q) * 2 + h // 2) * OWN, OWN)
                turned[h % 2, 0, pl.ds(to, OWN), :] = a
                turned[h % 2, 1, pl.ds(to, OWN), :] = b


def joined(values):
    top = jnp.max(values, axis=0)
    return top + jnp.log(jnp.sum(jnp.exp(values - top[None]), axis=0))


def column_bias(got, dblk):
    values = got[...]
    total = jnp.sum(values[:, CB, :], axis=0, keepdims=True)
    level = joined(values)
    parts = [-(level[k : k + 1, :] - jnp.log(total)) for k in range(CB)]
    return jnp.where(live_columns(dblk), jnp.concatenate(parts, axis=1), -jnp.inf)


def row_body(dblk, got, cost, out):
    bias = column_bias(got, dblk)
    eye = diagonal()
    out[...] = jnp.zeros((LROWS, BLOCK), F32)
    for k in range(RB):
        out[k : k + 1, :] = to_row(row_lse(cost, bias, k), eye)
    store_count(out, RB, dblk[0])


def column_body(nblk, got, cost, out, dual, column):
    values = got[...]
    total = jnp.sum(values[:, RB, :], axis=0, keepdims=True)
    duals = -(joined(values) - jnp.log(total))
    dual[...] = duals
    eye = diagonal()
    tops = []
    for k in range(RB):
        row = jnp.where(k < nblk[0], duals[k : k + 1, :], -jnp.inf)
        bias = to_column(row, eye)
        column[k * BLOCK : (k + 1) * BLOCK, :] = bias
        scores = bias - cost[k * BLOCK : (k + 1) * BLOCK, :]
        tops.append(jnp.max(scores.reshape(BLOCK // 8, 8, COLS), axis=0))
    top = tops[0]
    for k in range(1, RB):
        top = jnp.maximum(top, tops[k])
    top = jnp.max(top, axis=0, keepdims=True)
    mass = jnp.zeros((8, COLS), F32)
    for k in range(RB):
        part = slice(k * BLOCK, (k + 1) * BLOCK)
        scores = jnp.exp(column[part, :] - cost[part, :] - top)
        mass += jnp.sum(scores.reshape(BLOCK // 8, 8, COLS), axis=0)
    level = top + jnp.log(jnp.sum(mass, axis=0, keepdims=True))
    value = jnp.concatenate(
        [level[:, k * BLOCK : (k + 1) * BLOCK] for k in range(CB)]
        + [jnp.full((1, BLOCK), (nblk[0] * BLOCK).astype(F32))]
        + [jnp.zeros((8 - CB - 1, BLOCK), F32)],
        axis=0,
    )
    for z in range(NZ):
        out[z] = value


def project_noise_body(place, nblk, own, dual, cost, turned_high, turned_low, *refs):
    stay, away, whole, th, tl, weights_high, weights_low, sems = refs
    copies = [
        pltpu.make_async_copy(turned_high, th, sems.at[0]),
        pltpu.make_async_copy(turned_low, tl, sems.at[1]),
    ]
    for copy in copies:
        copy.start()
    level = jnp.concatenate([own[0, k : k + 1, :] for k in range(CB)], axis=1)
    eye = diagonal()
    for k in range(RB):
        part = slice(k * BLOCK, (k + 1) * BLOCK)
        row = jnp.where(k < nblk[0], dual[k : k + 1, :], -jnp.inf)
        a, b = halves(jnp.exp(to_column(row, eye) - cost[part, :] - level))
        weights_high[part, :] = a
        weights_low[part, :] = b
    for copy in copies:
        copy.wait()
    both = (weights_high[...], weights_low[...])
    for k in range(0, DIM, 256):
        some = dot3((th[k : k + 256, :], tl[k : k + 256, :]), both, ((1,), (0,)))
        for q in range(256 // CHUNK):
            for c in range(CB):
                whole[k // CHUNK + q, c * CHUNK : (c + 1) * CHUNK, :] = some[
                    q * CHUNK : (q + 1) * CHUNK, c * BLOCK : (c + 1) * BLOCK
                ]
    z = place[0]
    moves = []
    for q in range(NZ // 2):
        for n, (source, out) in enumerate(((neighbour(z), away), (z, stay))):
            take = whole.at[lax.rem(source + 2 * q, NZ)]
            moves.append(pltpu.make_async_copy(take, out.at[q], sems.at[2 + 2 * q + n]))
    for move in moves:
        move.start()
    for move in moves:
        move.wait()


def spread(out, some, k):
    for p in range(NXY):
        for h in range(2):
            out[p, (k * 2 + h) * OWN : (k * 2 + h + 1) * OWN, :] = some[
                p * OWN : (p + 1) * OWN, h * BLOCK : (h + 1) * BLOCK
            ]


def project_data_body(core, dblk, got, cost, turned, out, high, low, dual, tops):
    bias = column_bias(got, dblk)
    dual[...] = bias
    eye = diagonal()
    for k in range(RB):
        part = slice(k * BLOCK, (k + 1) * BLOCK)
        scores = bias - cost[part, :]
        top = jnp.max(scores, axis=1, keepdims=True)
        weights = jnp.exp(scores - top)
        level = top + jnp.log(jnp.sum(weights, axis=1, keepdims=True))
        tops[k : k + 1, :] = to_row(top, eye)
        tops[RB + k : RB + k + 1, :] = to_row(level, eye)
        a, b = halves(weights)
        high[part, :] = a
        low[part, :] = b
    other = 1 - core[0]
    for k in range(ROWS // 256):
        part = slice(k * 256, (k + 1) * 256)
        some = dot3((turned[other, 0], turned[other, 1]), (high[part, :], low[part, :]), ((1,), (1,)))
        spread(out, some, k)
    for p in range(NXY):
        out[p, TOPS:PIECE, :] = tops[...]


def project_own_body(core, turned, high, low, out):
    mine = core[0]
    for k in range(ROWS // 256):
        part = slice(k * 256, (k + 1) * 256)
        some = dot3((turned[mine, 0], turned[mine, 1]), (high[part, :], low[part, :]), ((1,), (1,)))
        spread(out, some, k)


def merge_body(own, own_tops, came, out):
    a, b = own_tops[RB : 2 * RB, :], came[0, LEVELS:PIECE, :]
    top = jnp.maximum(a, b)
    level = top + jnp.log(jnp.exp(a - top) + jnp.exp(b - top))
    a, b = jnp.exp(own_tops[0:RB, :] - level), jnp.exp(came[0, TOPS:LEVELS, :] - level)
    for k in range(RB):
        part = slice(k * OWN, (k + 1) * OWN)
        out[:, part, :] = (
            own[:, part, :] * a[k : k + 1, :][None] + came[:, part, :] * b[k : k + 1, :][None]
        )
    for p in range(NXY):
        out[p, LEVELS:PIECE, :] = level
        out[p, TOPS:LEVELS, :] = level


def finish_noise_body(nblk, came, out):
    levels = came[:, LEVELS:PIECE, :]
    shares = jnp.exp(levels - joined(levels)[None])
    for k in range(RB):
        part = slice(k * OWN, (k + 1) * OWN)
        total = jnp.sum(came[:, part, :] * shares[:, k : k + 1, :], axis=0)
        out[:, k * BLOCK : (k + 1) * BLOCK] = jnp.where(k < nblk[0], total, 0.0)


def pair_body(place, got, stay, came, *outs):
    level = joined(got[...])
    a = jnp.exp(got[place[0]] - level)
    b = jnp.exp(got[neighbour(place[0])] - level)
    for q in range(NZ // 2):
        for k in range(CB):
            part = slice(k * CHUNK, (k + 1) * CHUNK)
            outs[q][part, :] = stay[q, part, :] * a[k : k + 1, :] + came[q, part, :] * b[k : k + 1, :]


def finish_data_body(dblk, *refs):
    came, out = refs[: NZ // 2], refs[NZ // 2]
    for k in range(CB):
        part = slice(k * CHUNK, (k + 1) * CHUNK)
        total = (came[0][part, :] + came[1][part, :]) + (came[2][part, :] + came[3][part, :])
        out[:, k * BLOCK : (k + 1) * BLOCK] = jnp.where(k < dblk[0], total, 0.0)


CORES = [(0, 1), (1, 0)]
PAIRS = [(i, i ^ 1) for i in range(NZ)]


def over_dp(lse):
    came = lax.ppermute(lse, "c", CORES)
    top = jnp.maximum(lse, came)
    both = top + jnp.log(jnp.exp(lse - top) + jnp.exp(came - top))
    counts = lax.broadcasted_iota(jnp.int32, (LROWS, BLOCK), 0) == RB
    both = jnp.where(counts, lse + came, both)
    return lax.all_to_all(
        jnp.broadcast_to(both[None], (NXY, LROWS, BLOCK)), ("x", "y"), 0, 0, tiled=True
    )


def over_noise(pieces):
    return lax.all_to_all(pieces, "z", 0, 0, tiled=True)


def on_device(noise_points, data_points, noise_blocks, data_blocks):
    place = lax.axis_index("z").reshape(1)
    core = lax.axis_index("c").reshape(1)
    mine, place, core = lax.optimization_barrier((data_points.T, place, core))
    four = jnp.concatenate(
        [mine]
        + [lax.ppermute(mine, "z", [(i, (i + 2 * q) % NZ) for i in range(NZ)]) for q in (1, 2, 3)]
    )
    other = lax.ppermute(four, "z", PAIRS)
    high, low, turned_high, turned_low, squares = call(
        prepare_body,
        (
            shaped((2, ROWS, DIM // 2), BF16),
            shaped((2, ROWS, DIM // 2), BF16),
            pltpu.HBM((DIM, ROWS), BF16),
            pltpu.HBM((DIM, ROWS), BF16),
            shaped((ROWS, 1)),
        ),
        [SMEM] * 4 + [VMEM],
        [
            pltpu.VMEM((DIM, ROWS), BF16),
            pltpu.VMEM((DIM, ROWS), BF16),
            pltpu.SemaphoreType.DMA((2,)),
        ],
        limit=8,
        places=(VMEM, VMEM, HBM, HBM, VMEM),
    )(place, core, noise_blocks, data_blocks, noise_points)
    near = call(
        near_body,
        shaped((ROWS, COLS)),
        [SMEM] + [VMEM] * 4,
        [pltpu.VMEM((DIM // 2, COLS), BF16), pltpu.VMEM((DIM // 2, COLS), BF16)],
        limit=6,
    )(place, high, low, squares, four)
    cost, lse, turned = call(
        cost_body,
        (shaped((ROWS, COLS)), shaped((LROWS, BLOCK)), shaped((NC, 2, DIM // NC, COLS), BF16)),
        [SMEM, SMEM] + [VMEM] * 5,
        [pltpu.VMEM((DIM // 2, COLS), BF16), pltpu.VMEM((DIM // 2, COLS), BF16)],
        limit=6,
    )(place, data_blocks, high, low, four, other, near)
    for turn in range(ITERS):
        if turn:
            lse = call(row_body, shaped((LROWS, BLOCK)), [SMEM, VMEM, VMEM])(data_blocks, got, cost)
        rows = over_dp(lse)
        sent, dual = call(
            column_body,
            (shaped((NZ, 8, BLOCK)), shaped((LROWS, BLOCK))),
            [SMEM, VMEM, VMEM],
            [pltpu.VMEM((ROWS, 1), F32)],
        )(noise_blocks, rows, cost)
        got = over_noise(sent)
    stay, away = call(
        project_noise_body,
        [pltpu.HBM((NZ // 2, CB * CHUNK, BLOCK), F32) for _ in range(2)],
        [SMEM, SMEM, VMEM, VMEM, VMEM, HBM, HBM],
        [
            pltpu.VMEM((NZ, CB * CHUNK, BLOCK), F32),
            pltpu.VMEM((DIM, ROWS), BF16),
            pltpu.VMEM((DIM, ROWS), BF16),
            pltpu.VMEM((ROWS, COLS), BF16),
            pltpu.VMEM((ROWS, COLS), BF16),
            pltpu.SemaphoreType.DMA((2 + NZ,)),
        ],
        places=[HBM] * 2,
    )(
        place,
        noise_blocks,
        sent,
        dual,
        cost,
        pltpu.with_memory_space_constraint(turned_high, pltpu.HBM),
        pltpu.with_memory_space_constraint(turned_low, pltpu.HBM),
    )
    got, stay, away = lax.optimization_barrier((got, stay, away))
    paired = lax.ppermute(away, "z", PAIRS)
    summed = call(
        pair_body, [shaped((CB * CHUNK, BLOCK)) for _ in range(NZ // 2)], [SMEM, VMEM, VMEM, VMEM]
    )(place, got, stay, paired)
    data_came = [summed[0]] + [
        lax.ppermute(summed[q], "z", [(i, (i + 2 * q) % NZ) for i in range(NZ)])
        for q in (1, 2, 3)
    ]
    theirs, weights_high, weights_low, data_dual, level = call(
        project_data_body,
        (
            shaped((NXY, PIECE, BLOCK)),
            shaped((ROWS, COLS), BF16),
            shaped((ROWS, COLS), BF16),
            shaped((1, COLS)),
            shaped((2 * RB, BLOCK)),
        ),
        [SMEM, SMEM, VMEM, VMEM, VMEM],
    )(core, data_blocks, got, cost, turned)
    came = lax.ppermute(theirs, "c", CORES)
    own = call(
        project_own_body, shaped((NXY, RB * OWN, BLOCK)), [SMEM, VMEM, VMEM, VMEM]
    )(core, turned, weights_high, weights_low)
    merged = call(merge_body, shaped((NXY, PIECE, BLOCK)), [VMEM] * 3)(own, level, came)
    noise_came = lax.all_to_all(merged, ("x", "y"), 0, 0, tiled=True)
    noise_target = call(finish_noise_body, shaped((OWN, ROWS)), [SMEM, VMEM])(
        noise_blocks, noise_came
    )
    data_target = call(
        finish_data_body, shaped((CHUNK, COLS)), [SMEM] + [VMEM] * (NZ // 2)
    )(data_blocks, *data_came)
    row_live = jnp.arange(ROWS, dtype=jnp.int32) < noise_blocks[0] * BLOCK
    column_live = jnp.arange(COLS, dtype=jnp.int32) < data_blocks[0] * BLOCK
    noise_potential = jnp.where(row_live, SMOOTHING_TEMP * dual[:RB].reshape(ROWS), 0.0)
    data_potential = jnp.where(column_live, SMOOTHING_TEMP * data_dual.reshape(COLS), 0.0)
    return noise_potential, data_potential, noise_target, data_target


def solution(mesh):
    axes = Mesh(mesh.devices.reshape(NZ, 4, 4, NC), ("z", "x", "y", "c"))
    dp = ("x", "y", "c")
    return jax.shard_map(
        on_device,
        mesh=axes,
        in_specs=(P("z", None), P(dp, "z"), P("z"), P(dp)),
        out_specs=(P("z"), P(dp), P(dp, "z"), P("z", dp)),
        check_vma=False,
    )
```

```python
import jax
import jax.numpy as jnp
from jax import lax
from jax.experimental import pallas as pl
from jax.experimental.pallas import tpu as pltpu
from jax.sharding import Mesh, PartitionSpec as P


BLOCK = 128
ITERS = 3
SMOOTHING_TEMP = 0.125
SHARP = 1.0 / SMOOTHING_TEMP

F32 = jnp.float32
BF16 = jnp.bfloat16
NZ, NXY, NC = 8, 16, 2
ROWS, COLS, DIM = 1536, 384, 512
RB, CB = ROWS // BLOCK, COLS // BLOCK
CHUNK = DIM // NZ
OWN = DIM // (NXY * NC)
LROWS = 16
TOPS = RB * OWN
LEVELS = TOPS + RB
PIECE = TOPS + 2 * RB
SENT = TOPS + LROWS

SMEM = pl.BlockSpec(memory_space=pltpu.SMEM)
VMEM = pl.BlockSpec(memory_space=pltpu.VMEM)
HBM = pl.BlockSpec(memory_space=pltpu.HBM)


def shaped(shape, dtype=F32):
    return jax.ShapeDtypeStruct(shape, dtype)


def call(body, outs, ins, scratch=(), limit=16, places=None):
    return pl.pallas_call(
        body,
        out_shape=outs,
        in_specs=ins,
        out_specs=places or jax.tree.map(lambda _: VMEM, outs),
        scratch_shapes=scratch,
        cost_estimate=pl.CostEstimate(flops=1000000, transcendentals=0, bytes_accessed=4000000),
        compiler_params=pltpu.CompilerParams(vmem_limit_bytes=limit << 20),
    )


def halves(value):
    high = value.astype(BF16)
    return high, (value - high.astype(F32)).astype(BF16)


def dot(a, b, dims):
    return lax.dot_general(a, b, (dims, ((), ())), preferred_element_type=F32)


def dot3(a, b, dims):
    return dot(a[0], b[0], dims) + (dot(a[0], b[1], dims) + dot(a[1], b[0], dims))


def diagonal():
    return lax.broadcasted_iota(jnp.int32, (BLOCK, BLOCK), 0) == lax.broadcasted_iota(
        jnp.int32, (BLOCK, BLOCK), 1
    )


def to_row(column, eye):
    return jnp.sum(jnp.where(eye, column, 0.0), axis=0, keepdims=True)


def to_column(row, eye):
    return jnp.sum(jnp.where(eye, jnp.broadcast_to(row, (BLOCK, BLOCK)), 0.0), axis=1, keepdims=True)


def prepare_body(
    place, core, nblk, dblk, points, high, low, turned_high, turned_low, squares, th, tl, sems
):
    for k in range(0, ROWS, 256):
        part = points[k : k + 256, :]
        squares[k : k + 256, :] = jnp.sum(part * part, axis=1, keepdims=True)
        a, b = halves(part)
        for p in range(2):
            for q in range(NZ // 2):
                take = slice((2 * q + p) * CHUNK, (2 * q + p + 1) * CHUNK)
                high[p, k : k + 256, q * CHUNK : (q + 1) * CHUNK] = a[:, take]
                low[p, k : k + 256, q * CHUNK : (q + 1) * CHUNK] = b[:, take]
        a, b = halves(part.T)
        th[:, k : k + 256] = a
        tl[:, k : k + 256] = b
    copies = [
        pltpu.make_async_copy(th, turned_high, sems.at[0]),
        pltpu.make_async_copy(tl, turned_low, sems.at[1]),
    ]
    for copy in copies:
        copy.start()
    for copy in copies:
        copy.wait()


def row_lse(cost, bias, k):
    scores = bias - cost[k * BLOCK : (k + 1) * BLOCK, :]
    top = jnp.max(scores, axis=1, keepdims=True)
    return top + jnp.log(jnp.sum(jnp.exp(scores - top), axis=1, keepdims=True))


def live_columns(dblk):
    return lax.broadcasted_iota(jnp.int32, (1, COLS), 1) < dblk[0] * BLOCK


def store_count(out, row, count):
    out[row : row + 1, :] = jnp.full((1, BLOCK), (count * BLOCK).astype(F32))


def neighbour(z):
    return z + 1 - 2 * lax.rem(z, 2)


def near_pieces(z, refs):
    return [(lax.rem(z + (NZ - 2 * q), NZ), refs[q][...]) for q in range(NZ // 2)]


def far_pieces(z, left, right):
    return [
        (lax.rem(z + shift, NZ), side[h * CHUNK : (h + 1) * CHUNK, :])
        for side, shifts in ((left, (NZ - 1, NZ - 3)), (right, (1, 3)))
        for h, shift in enumerate(shifts)
    ]


def half_product(side, pieces, high, low, data_high, data_low):
    square = jnp.zeros((1, COLS), F32)
    for source, piece in pieces:
        square += jnp.sum(piece * piece, axis=0, keepdims=True)
        a, b = halves(piece)
        at = pl.multiple_of(lax.div(source, 2) * CHUNK, CHUNK)
        data_high[pl.ds(at, CHUNK), :] = a
        data_low[pl.ds(at, CHUNK), :] = b
    both = (data_high[...], data_low[...])

    def cross(k):
        part = slice(k, k + 256)
        return square - 2.0 * dot3((high[side, part, :], low[side, part, :]), both, ((1,), (0,)))

    return cross


def turn(turned, pieces):
    for source, piece in pieces:
        for h in range(CHUNK // OWN):
            a, b = halves(piece[h * OWN : (h + 1) * OWN, :])
            to = pl.multiple_of((source * 2 + h // 2) * OWN, OWN)
            turned[h % 2, 0, pl.ds(to, OWN), :] = a
            turned[h % 2, 1, pl.ds(to, OWN), :] = b


def near_body(place, high, low, squares, *refs):
    pieces, (cost, data_high, data_low) = near_pieces(place[0], refs[:4]), refs[4:]
    cross = half_product(lax.rem(place[0], 2), pieces, high, low, data_high, data_low)
    for k in range(0, ROWS, 256):
        cost[k : k + 256, :] = squares[k : k + 256, :] + cross(k)


def cost_body(place, dblk, high, low, near, left, right, *refs):
    z, own, (cost, out, turned, data_high, data_low) = place[0], refs[:4], refs[4:]
    pieces = far_pieces(z, left, right)
    cross = half_product(1 - lax.rem(z, 2), pieces, high, low, data_high, data_low)
    eye = diagonal()
    bias = jnp.where(live_columns(dblk), 0.0, -jnp.inf)
    out[...] = jnp.zeros((LROWS, BLOCK), F32)
    for k in range(0, ROWS, 256):
        cost[k : k + 256, :] = SHARP * (near[k : k + 256, :] + cross(k))
    for k in range(RB):
        out[k : k + 1, :] = to_row(row_lse(cost, bias, k), eye)
    store_count(out, RB, dblk[0])
    turn(turned, pieces + near_pieces(z, own))


def joined(values):
    top = jnp.max(values, axis=0)
    return top + jnp.log(jnp.sum(jnp.exp(values - top[None]), axis=0))


def column_bias(got, dblk):
    values = got[...]
    total = jnp.sum(values[:, CB, :], axis=0, keepdims=True)
    level = joined(values)
    parts = [-(level[k : k + 1, :] - jnp.log(total)) for k in range(CB)]
    return jnp.where(live_columns(dblk), jnp.concatenate(parts, axis=1), -jnp.inf)


def row_body(dblk, got, cost, out):
    bias = column_bias(got, dblk)
    eye = diagonal()
    out[...] = jnp.zeros((LROWS, BLOCK), F32)
    for k in range(RB):
        out[k : k + 1, :] = to_row(row_lse(cost, bias, k), eye)
    store_count(out, RB, dblk[0])


def column_body(nblk, got, cost, out, dual, column):
    values = got[...]
    total = jnp.sum(values[:, RB, :], axis=0, keepdims=True)
    duals = -(joined(values) - jnp.log(total))
    dual[...] = duals
    eye = diagonal()
    tops = []
    for k in range(RB):
        row = jnp.where(k < nblk[0], duals[k : k + 1, :], -jnp.inf)
        bias = to_column(row, eye)
        column[k * BLOCK : (k + 1) * BLOCK, :] = bias
        scores = bias - cost[k * BLOCK : (k + 1) * BLOCK, :]
        tops.append(jnp.max(scores.reshape(BLOCK // 8, 8, COLS), axis=0))
    top = tops[0]
    for k in range(1, RB):
        top = jnp.maximum(top, tops[k])
    top = jnp.max(top, axis=0, keepdims=True)
    mass = jnp.zeros((8, COLS), F32)
    for k in range(RB):
        part = slice(k * BLOCK, (k + 1) * BLOCK)
        scores = jnp.exp(column[part, :] - cost[part, :] - top)
        mass += jnp.sum(scores.reshape(BLOCK // 8, 8, COLS), axis=0)
    level = top + jnp.log(jnp.sum(mass, axis=0, keepdims=True))
    value = jnp.concatenate(
        [level[:, k * BLOCK : (k + 1) * BLOCK] for k in range(CB)]
        + [jnp.full((1, BLOCK), (nblk[0] * BLOCK).astype(F32))]
        + [jnp.zeros((8 - CB - 1, BLOCK), F32)],
        axis=0,
    )
    for z in range(NZ):
        out[z] = value


def project_noise_body(place, nblk, own, dual, cost, turned_high, turned_low, *refs):
    stay, away, whole, th, tl, weights_high, weights_low, sems = refs
    copies = [
        pltpu.make_async_copy(turned_high, th, sems.at[0]),
        pltpu.make_async_copy(turned_low, tl, sems.at[1]),
    ]
    for copy in copies:
        copy.start()
    level = jnp.concatenate([own[0, k : k + 1, :] for k in range(CB)], axis=1)
    eye = diagonal()
    for k in range(RB):
        part = slice(k * BLOCK, (k + 1) * BLOCK)
        row = jnp.where(k < nblk[0], dual[k : k + 1, :], -jnp.inf)
        a, b = halves(jnp.exp(to_column(row, eye) - cost[part, :] - level))
        weights_high[part, :] = a
        weights_low[part, :] = b
    for copy in copies:
        copy.wait()
    both = (weights_high[...], weights_low[...])
    for k in range(0, DIM, 256):
        some = dot3((th[k : k + 256, :], tl[k : k + 256, :]), both, ((1,), (0,)))
        for q in range(256 // CHUNK):
            for c in range(CB):
                whole[k // CHUNK + q, c * CHUNK : (c + 1) * CHUNK, :] = some[
                    q * CHUNK : (q + 1) * CHUNK, c * BLOCK : (c + 1) * BLOCK
                ]
    z = place[0]
    moves = []
    for q in range(NZ // 2):
        for n, (source, out) in enumerate(((neighbour(z), away), (z, stay))):
            take = whole.at[lax.rem(source + 2 * q, NZ)]
            moves.append(pltpu.make_async_copy(take, out.at[q], sems.at[2 + 2 * q + n]))
    for move in moves:
        move.start()
    for move in moves:
        move.wait()


def spread(out, some, k):
    for p in range(NXY):
        for h in range(2):
            out[p, (k * 2 + h) * OWN : (k * 2 + h + 1) * OWN, :] = some[
                p * OWN : (p + 1) * OWN, h * BLOCK : (h + 1) * BLOCK
            ]


def project_data_body(core, dblk, got, cost, turned, out, high, low, dual, tops):
    bias = column_bias(got, dblk)
    dual[...] = bias
    eye = diagonal()
    for k in range(RB):
        part = slice(k * BLOCK, (k + 1) * BLOCK)
        scores = bias - cost[part, :]
        top = jnp.max(scores, axis=1, keepdims=True)
        weights = jnp.exp(scores - top)
        level = top + jnp.log(jnp.sum(weights, axis=1, keepdims=True))
        tops[k : k + 1, :] = to_row(top, eye)
        tops[RB + k : RB + k + 1, :] = to_row(level, eye)
        a, b = halves(weights)
        high[part, :] = a
        low[part, :] = b
    other = 1 - core[0]
    for k in range(ROWS // 256):
        part = slice(k * 256, (k + 1) * 256)
        some = dot3((turned[other, 0], turned[other, 1]), (high[part, :], low[part, :]), ((1,), (1,)))
        spread(out, some, k)
    for p in range(NXY):
        out[p, TOPS:PIECE, :] = tops[...]


def project_own_body(core, turned, high, low, out):
    mine = core[0]
    for k in range(ROWS // 256):
        part = slice(k * 256, (k + 1) * 256)
        some = dot3((turned[mine, 0], turned[mine, 1]), (high[part, :], low[part, :]), ((1,), (1,)))
        spread(out, some, k)


def merge_body(own, own_tops, came, out):
    a, b = own_tops[RB : 2 * RB, :], came[0, LEVELS:PIECE, :]
    top = jnp.maximum(a, b)
    level = top + jnp.log(jnp.exp(a - top) + jnp.exp(b - top))
    a, b = jnp.exp(own_tops[0:RB, :] - level), jnp.exp(came[0, TOPS:LEVELS, :] - level)
    for k in range(RB):
        part = slice(k * OWN, (k + 1) * OWN)
        out[:, part, :] = (
            own[:, part, :] * a[k : k + 1, :][None] + came[:, part, :] * b[k : k + 1, :][None]
        )
    for p in range(NXY):
        out[p, TOPS : TOPS + RB, :] = level
        out[p, TOPS + RB : SENT, :] = level[0 : SENT - TOPS - RB, :]


def finish_noise_body(nblk, came, out):
    levels = came[:, TOPS : TOPS + RB, :]
    shares = jnp.exp(levels - joined(levels)[None])
    for k in range(RB):
        part = slice(k * OWN, (k + 1) * OWN)
        total = jnp.sum(came[:, part, :] * shares[:, k : k + 1, :], axis=0)
        out[:, k * BLOCK : (k + 1) * BLOCK] = jnp.where(k < nblk[0], total, 0.0)


def pair_body(place, got, stay, came, *outs):
    level = joined(got[...])
    a = jnp.exp(got[place[0]] - level)
    b = jnp.exp(got[neighbour(place[0])] - level)
    for q in range(NZ // 2):
        for k in range(CB):
            part = slice(k * CHUNK, (k + 1) * CHUNK)
            outs[q][part, :] = stay[q, part, :] * a[k : k + 1, :] + came[q, part, :] * b[k : k + 1, :]


def finish_data_body(dblk, *refs):
    came, out = refs[: NZ // 2], refs[NZ // 2]
    for k in range(CB):
        part = slice(k * CHUNK, (k + 1) * CHUNK)
        total = (came[0][part, :] + came[1][part, :]) + (came[2][part, :] + came[3][part, :])
        out[:, k * BLOCK : (k + 1) * BLOCK] = jnp.where(k < dblk[0], total, 0.0)


CORES = [(0, 1), (1, 0)]
PAIRS = [(i, i ^ 1) for i in range(NZ)]


def shifted(s):
    return [(i, (i + s) % NZ) for i in range(NZ)]


def over_dp(lse):
    came = lax.ppermute(lse, "c", CORES)
    top = jnp.maximum(lse, came)
    both = top + jnp.log(jnp.exp(lse - top) + jnp.exp(came - top))
    counts = lax.broadcasted_iota(jnp.int32, (LROWS, BLOCK), 0) == RB
    both = jnp.where(counts, lse + came, both)
    return lax.all_to_all(
        jnp.broadcast_to(both[None], (NXY, LROWS, BLOCK)), ("x", "y"), 0, 0, tiled=True
    )


def over_noise(pieces):
    return lax.all_to_all(pieces, "z", 0, 0, tiled=True)


def on_device(noise_points, data_points, noise_blocks, data_blocks):
    place = lax.axis_index("z").reshape(1)
    core = lax.axis_index("c").reshape(1)
    mine, place, core = lax.optimization_barrier((data_points.T, place, core))
    own = [mine] + [lax.ppermute(mine, "z", shifted(2 * q)) for q in (1, 2, 3)]
    left = lax.ppermute(jnp.concatenate([mine, own[1]]), "z", shifted(1))
    right = lax.ppermute(jnp.concatenate([mine, own[3]]), "z", shifted(NZ - 1))
    high, low, turned_high, turned_low, squares = call(
        prepare_body,
        (
            shaped((2, ROWS, DIM // 2), BF16),
            shaped((2, ROWS, DIM // 2), BF16),
            pltpu.HBM((DIM, ROWS), BF16),
            pltpu.HBM((DIM, ROWS), BF16),
            shaped((ROWS, 1)),
        ),
        [SMEM] * 4 + [VMEM],
        [
            pltpu.VMEM((DIM, ROWS), BF16),
            pltpu.VMEM((DIM, ROWS), BF16),
            pltpu.SemaphoreType.DMA((2,)),
        ],
        limit=8,
        places=(VMEM, VMEM, HBM, HBM, VMEM),
    )(place, core, noise_blocks, data_blocks, noise_points)
    near = call(
        near_body,
        shaped((ROWS, COLS)),
        [SMEM] + [VMEM] * 7,
        [pltpu.VMEM((DIM // 2, COLS), BF16), pltpu.VMEM((DIM // 2, COLS), BF16)],
        limit=6,
    )(place, high, low, squares, *own)
    cost, lse, turned = call(
        cost_body,
        (shaped((ROWS, COLS)), shaped((LROWS, BLOCK)), shaped((NC, 2, DIM // NC, COLS), BF16)),
        [SMEM, SMEM] + [VMEM] * 9,
        [pltpu.VMEM((DIM // 2, COLS), BF16), pltpu.VMEM((DIM // 2, COLS), BF16)],
        limit=6,
    )(place, data_blocks, high, low, near, left, right, *own)
    for turn in range(ITERS):
        if turn:
            lse = call(row_body, shaped((LROWS, BLOCK)), [SMEM, VMEM, VMEM])(data_blocks, got, cost)
        rows = over_dp(lse)
        sent, dual = call(
            column_body,
            (shaped((NZ, 8, BLOCK)), shaped((LROWS, BLOCK))),
            [SMEM, VMEM, VMEM],
            [pltpu.VMEM((ROWS, 1), F32)],
        )(noise_blocks, rows, cost)
        got = over_noise(sent)
    stay, away = call(
        project_noise_body,
        [pltpu.HBM((NZ // 2, CB * CHUNK, BLOCK), F32) for _ in range(2)],
        [SMEM, SMEM, VMEM, VMEM, VMEM, HBM, HBM],
        [
            pltpu.VMEM((NZ, CB * CHUNK, BLOCK), F32),
            pltpu.VMEM((DIM, ROWS), BF16),
            pltpu.VMEM((DIM, ROWS), BF16),
            pltpu.VMEM((ROWS, COLS), BF16),
            pltpu.VMEM((ROWS, COLS), BF16),
            pltpu.SemaphoreType.DMA((2 + NZ,)),
        ],
        places=[HBM] * 2,
    )(
        place,
        noise_blocks,
        sent,
        dual,
        cost,
        pltpu.with_memory_space_constraint(turned_high, pltpu.HBM),
        pltpu.with_memory_space_constraint(turned_low, pltpu.HBM),
    )
    got, stay, away = lax.optimization_barrier((got, stay, away))
    paired = lax.ppermute(away, "z", PAIRS)
    summed = call(
        pair_body, [shaped((CB * CHUNK, BLOCK)) for _ in range(NZ // 2)], [SMEM, VMEM, VMEM, VMEM]
    )(
        place,
        got,
        pltpu.with_memory_space_constraint(stay, pltpu.HBM),
        pltpu.with_memory_space_constraint(paired, pltpu.HBM),
    )
    data_came = [summed[0]] + [
        lax.ppermute(summed[q], "z", shifted(2 * q)) for q in (1, 2, 3)
    ]
    theirs, weights_high, weights_low, data_dual, level = call(
        project_data_body,
        (
            shaped((NXY, PIECE, BLOCK)),
            shaped((ROWS, COLS), BF16),
            shaped((ROWS, COLS), BF16),
            shaped((1, COLS)),
            shaped((2 * RB, BLOCK)),
        ),
        [SMEM, SMEM, VMEM, VMEM, VMEM],
    )(core, data_blocks, got, cost, turned)
    came = lax.ppermute(theirs, "c", CORES)
    own = call(
        project_own_body, shaped((NXY, RB * OWN, BLOCK)), [SMEM, VMEM, VMEM, VMEM]
    )(core, turned, weights_high, weights_low)
    merged = call(merge_body, pltpu.VMEM((NXY, SENT, BLOCK), F32), [VMEM] * 3)(own, level, came)
    noise_came = lax.all_to_all(merged, ("x", "y"), 0, 0, tiled=True)
    noise_target = call(finish_noise_body, shaped((OWN, ROWS)), [SMEM, VMEM])(
        noise_blocks, noise_came
    )
    data_target = call(
        finish_data_body, shaped((CHUNK, COLS)), [SMEM] + [VMEM] * (NZ // 2)
    )(data_blocks, *data_came)
    row_live = jnp.arange(ROWS, dtype=jnp.int32) < noise_blocks[0] * BLOCK
    column_live = jnp.arange(COLS, dtype=jnp.int32) < data_blocks[0] * BLOCK
    noise_potential = jnp.where(row_live, SMOOTHING_TEMP * dual[:RB].reshape(ROWS), 0.0)
    data_potential = jnp.where(column_live, SMOOTHING_TEMP * data_dual.reshape(COLS), 0.0)
    return noise_potential, data_potential, noise_target, data_target


def solution(mesh):
    axes = Mesh(mesh.devices.reshape(NZ, 4, 4, NC), ("z", "x", "y", "c"))
    dp = ("x", "y", "c")
    return jax.shard_map(
        on_device,
        mesh=axes,
        in_specs=(P("z", None), P(dp, "z"), P("z"), P(dp)),
        out_specs=(P("z"), P(dp), P(dp, "z"), P("z", dp)),
        check_vma=False,
    )
```

```python
import jax
import jax.numpy as jnp
from jax import lax
from jax.experimental import pallas as pl
from jax.experimental.pallas import tpu as pltpu
from jax.sharding import Mesh, PartitionSpec as P


BLOCK = 128
ITERS = 3
SMOOTHING_TEMP = 0.125
SHARP = 1.0 / SMOOTHING_TEMP

F32 = jnp.float32
BF16 = jnp.bfloat16
NZ, NXY, NC = 8, 16, 2
ROWS, COLS, DIM = 1536, 384, 512
RB, CB = ROWS // BLOCK, COLS // BLOCK
CHUNK = DIM // NZ
OWN = DIM // (NXY * NC)
LROWS = 16
TOPS = RB * OWN
LEVELS = TOPS + RB
PIECE = TOPS + 2 * RB
SENT = TOPS + LROWS

SMEM = pl.BlockSpec(memory_space=pltpu.SMEM)
VMEM = pl.BlockSpec(memory_space=pltpu.VMEM)
HBM = pl.BlockSpec(memory_space=pltpu.HBM)


def shaped(shape, dtype=F32):
    return jax.ShapeDtypeStruct(shape, dtype)


def call(body, outs, ins, scratch=(), limit=16, places=None):
    return pl.pallas_call(
        body,
        out_shape=outs,
        in_specs=ins,
        out_specs=places or jax.tree.map(lambda _: VMEM, outs),
        scratch_shapes=scratch,
        cost_estimate=pl.CostEstimate(flops=1000000, transcendentals=0, bytes_accessed=4000000),
        compiler_params=pltpu.CompilerParams(vmem_limit_bytes=limit << 20),
    )


def halves(value):
    high = value.astype(BF16)
    return high, (value - high.astype(F32)).astype(BF16)


def dot(a, b, dims):
    return lax.dot_general(a, b, (dims, ((), ())), preferred_element_type=F32)


def dot3(a, b, dims):
    return dot(a[0], b[0], dims) + (dot(a[0], b[1], dims) + dot(a[1], b[0], dims))


def diagonal():
    return lax.broadcasted_iota(jnp.int32, (BLOCK, BLOCK), 0) == lax.broadcasted_iota(
        jnp.int32, (BLOCK, BLOCK), 1
    )


def to_row(column, eye):
    return jnp.sum(jnp.where(eye, column, 0.0), axis=0, keepdims=True)


def to_column(row, eye):
    return jnp.sum(jnp.where(eye, jnp.broadcast_to(row, (BLOCK, BLOCK)), 0.0), axis=1, keepdims=True)


def prepare_body(
    place, core, nblk, dblk, points, high, low, turned_high, turned_low, squares, rows, th, tl, sems
):
    parts = [slice(k, k + 256) for k in range(0, ROWS, 256)]
    loads = [
        pltpu.make_async_copy(points.at[part, :], rows.at[part, :], sems.at[0, n])
        for n, part in enumerate(parts)
    ]
    for load in loads:
        load.start()
    stores = []
    for n, part in enumerate(parts):
        loads[n].wait()
        some = rows[part, :]
        squares[part, :] = jnp.sum(some * some, axis=1, keepdims=True)
        a, b = halves(some)
        for p in range(2):
            for q in range(NZ // 2):
                take = slice((2 * q + p) * CHUNK, (2 * q + p + 1) * CHUNK)
                high[p, part, q * CHUNK : (q + 1) * CHUNK] = a[:, take]
                low[p, part, q * CHUNK : (q + 1) * CHUNK] = b[:, take]
        a, b = halves(some.T)
        th[:, part] = a
        tl[:, part] = b
        for m, (source, out) in enumerate(((th, turned_high), (tl, turned_low))):
            store = pltpu.make_async_copy(source.at[:, part], out.at[:, part], sems.at[1 + m, n])
            store.start()
            stores.append(store)
    for store in stores:
        store.wait()


def row_lse(cost, bias, k):
    scores = bias - cost[k * BLOCK : (k + 1) * BLOCK, :]
    top = jnp.max(scores, axis=1, keepdims=True)
    return top + jnp.log(jnp.sum(jnp.exp(scores - top), axis=1, keepdims=True))


def live_columns(dblk):
    return lax.broadcasted_iota(jnp.int32, (1, COLS), 1) < dblk[0] * BLOCK


def store_count(out, row, count):
    out[row : row + 1, :] = jnp.full((1, BLOCK), (count * BLOCK).astype(F32))


def neighbour(z):
    return z + 1 - 2 * lax.rem(z, 2)


def near_pieces(z, refs):
    return [(lax.rem(z + (NZ - 2 * q), NZ), refs[q][...]) for q in range(NZ // 2)]


def far_pieces(z, left, right):
    return [
        (lax.rem(z + shift, NZ), side[h * CHUNK : (h + 1) * CHUNK, :])
        for side, shifts in ((left, (NZ - 1, NZ - 3)), (right, (1, 3)))
        for h, shift in enumerate(shifts)
    ]


def half_product(side, pieces, high, low, data_high, data_low):
    square = jnp.zeros((1, COLS), F32)
    for source, piece in pieces:
        square += jnp.sum(piece * piece, axis=0, keepdims=True)
        a, b = halves(piece)
        at = pl.multiple_of(lax.div(source, 2) * CHUNK, CHUNK)
        data_high[pl.ds(at, CHUNK), :] = a
        data_low[pl.ds(at, CHUNK), :] = b
    both = (data_high[...], data_low[...])

    def cross(k):
        part = slice(k, k + 256)
        return square - 2.0 * dot3((high[side, part, :], low[side, part, :]), both, ((1,), (0,)))

    return cross


def turn(turned, pieces):
    for source, piece in pieces:
        for h in range(CHUNK // OWN):
            a, b = halves(piece[h * OWN : (h + 1) * OWN, :])
            to = pl.multiple_of((source * 2 + h // 2) * OWN, OWN)
            turned[h % 2, 0, pl.ds(to, OWN), :] = a
            turned[h % 2, 1, pl.ds(to, OWN), :] = b


def near_body(place, high, low, squares, *refs):
    pieces, (cost, data_high, data_low) = near_pieces(place[0], refs[:4]), refs[4:]
    cross = half_product(lax.rem(place[0], 2), pieces, high, low, data_high, data_low)
    for k in range(0, ROWS, 256):
        cost[k : k + 256, :] = squares[k : k + 256, :] + cross(k)


def cost_body(place, dblk, high, low, near, left, right, *refs):
    z, own, (cost, out, turned, data_high, data_low) = place[0], refs[:4], refs[4:]
    pieces = far_pieces(z, left, right)
    cross = half_product(1 - lax.rem(z, 2), pieces, high, low, data_high, data_low)
    eye = diagonal()
    bias = jnp.where(live_columns(dblk), 0.0, -jnp.inf)
    out[...] = jnp.zeros((LROWS, BLOCK), F32)
    for k in range(0, ROWS, 256):
        cost[k : k + 256, :] = SHARP * (near[k : k + 256, :] + cross(k))
    for k in range(RB):
        out[k : k + 1, :] = to_row(row_lse(cost, bias, k), eye)
    store_count(out, RB, dblk[0])
    turn(turned, pieces + near_pieces(z, own))


def joined(values):
    top = jnp.max(values, axis=0)
    return top + jnp.log(jnp.sum(jnp.exp(values - top[None]), axis=0))


def column_bias(got, dblk):
    values = got[...]
    total = jnp.sum(values[:, CB, :], axis=0, keepdims=True)
    level = joined(values)
    parts = [-(level[k : k + 1, :] - jnp.log(total)) for k in range(CB)]
    return jnp.where(live_columns(dblk), jnp.concatenate(parts, axis=1), -jnp.inf)


def row_body(dblk, got, cost, out):
    bias = column_bias(got, dblk)
    eye = diagonal()
    out[...] = jnp.zeros((LROWS, BLOCK), F32)
    for k in range(RB):
        out[k : k + 1, :] = to_row(row_lse(cost, bias, k), eye)
    store_count(out, RB, dblk[0])


def column_body(nblk, got, cost, out, dual, column):
    values = got[...]
    total = jnp.sum(values[:, RB, :], axis=0, keepdims=True)
    duals = -(joined(values) - jnp.log(total))
    dual[...] = duals
    eye = diagonal()
    tops = []
    for k in range(RB):
        row = jnp.where(k < nblk[0], duals[k : k + 1, :], -jnp.inf)
        bias = to_column(row, eye)
        column[k * BLOCK : (k + 1) * BLOCK, :] = bias
        scores = bias - cost[k * BLOCK : (k + 1) * BLOCK, :]
        tops.append(jnp.max(scores.reshape(BLOCK // 8, 8, COLS), axis=0))
    top = tops[0]
    for k in range(1, RB):
        top = jnp.maximum(top, tops[k])
    top = jnp.max(top, axis=0, keepdims=True)
    mass = jnp.zeros((8, COLS), F32)
    for k in range(RB):
        part = slice(k * BLOCK, (k + 1) * BLOCK)
        scores = jnp.exp(column[part, :] - cost[part, :] - top)
        mass += jnp.sum(scores.reshape(BLOCK // 8, 8, COLS), axis=0)
    level = top + jnp.log(jnp.sum(mass, axis=0, keepdims=True))
    value = jnp.concatenate(
        [level[:, k * BLOCK : (k + 1) * BLOCK] for k in range(CB)]
        + [jnp.full((1, BLOCK), (nblk[0] * BLOCK).astype(F32))]
        + [jnp.zeros((8 - CB - 1, BLOCK), F32)],
        axis=0,
    )
    for z in range(NZ):
        out[z] = value


def project_noise_body(place, nblk, own, dual, cost, turned_high, turned_low, *refs):
    stay, away, whole, th, tl, weights_high, weights_low, sems = refs
    copies = [
        pltpu.make_async_copy(turned_high, th, sems.at[0]),
        pltpu.make_async_copy(turned_low, tl, sems.at[1]),
    ]
    for copy in copies:
        copy.start()
    level = jnp.concatenate([own[0, k : k + 1, :] for k in range(CB)], axis=1)
    eye = diagonal()
    for k in range(RB):
        part = slice(k * BLOCK, (k + 1) * BLOCK)
        row = jnp.where(k < nblk[0], dual[k : k + 1, :], -jnp.inf)
        a, b = halves(jnp.exp(to_column(row, eye) - cost[part, :] - level))
        weights_high[part, :] = a
        weights_low[part, :] = b
    for copy in copies:
        copy.wait()
    both = (weights_high[...], weights_low[...])
    for k in range(0, DIM, 256):
        some = dot3((th[k : k + 256, :], tl[k : k + 256, :]), both, ((1,), (0,)))
        for q in range(256 // CHUNK):
            for c in range(CB):
                whole[k // CHUNK + q, c * CHUNK : (c + 1) * CHUNK, :] = some[
                    q * CHUNK : (q + 1) * CHUNK, c * BLOCK : (c + 1) * BLOCK
                ]
    z = place[0]
    moves = []
    for q in range(NZ // 2):
        for n, (source, out) in enumerate(((neighbour(z), away), (z, stay))):
            take = whole.at[lax.rem(source + 2 * q, NZ)]
            moves.append(pltpu.make_async_copy(take, out.at[q], sems.at[2 + 2 * q + n]))
    for move in moves:
        move.start()
    for move in moves:
        move.wait()


def spread(out, some, k):
    for p in range(NXY):
        for h in range(2):
            out[p, (k * 2 + h) * OWN : (k * 2 + h + 1) * OWN, :] = some[
                p * OWN : (p + 1) * OWN, h * BLOCK : (h + 1) * BLOCK
            ]


def project_data_body(core, dblk, got, cost, turned, out, high, low, dual, tops):
    bias = column_bias(got, dblk)
    dual[...] = bias
    eye = diagonal()
    for k in range(RB):
        part = slice(k * BLOCK, (k + 1) * BLOCK)
        scores = bias - cost[part, :]
        top = jnp.max(scores, axis=1, keepdims=True)
        weights = jnp.exp(scores - top)
        level = top + jnp.log(jnp.sum(weights, axis=1, keepdims=True))
        tops[k : k + 1, :] = to_row(top, eye)
        tops[RB + k : RB + k + 1, :] = to_row(level, eye)
        a, b = halves(weights)
        high[part, :] = a
        low[part, :] = b
    other = 1 - core[0]
    for k in range(ROWS // 256):
        part = slice(k * 256, (k + 1) * 256)
        some = dot3((turned[other, 0], turned[other, 1]), (high[part, :], low[part, :]), ((1,), (1,)))
        spread(out, some, k)
    for p in range(NXY):
        out[p, TOPS:PIECE, :] = tops[...]


def project_own_body(core, turned, high, low, out):
    mine = core[0]
    for k in range(ROWS // 256):
        part = slice(k * 256, (k + 1) * 256)
        some = dot3((turned[mine, 0], turned[mine, 1]), (high[part, :], low[part, :]), ((1,), (1,)))
        spread(out, some, k)


def merge_body(own, own_tops, came, out):
    a, b = own_tops[RB : 2 * RB, :], came[0, LEVELS:PIECE, :]
    top = jnp.maximum(a, b)
    level = top + jnp.log(jnp.exp(a - top) + jnp.exp(b - top))
    a, b = jnp.exp(own_tops[0:RB, :] - level), jnp.exp(came[0, TOPS:LEVELS, :] - level)
    for k in range(RB):
        part = slice(k * OWN, (k + 1) * OWN)
        out[:, part, :] = (
            own[:, part, :] * a[k : k + 1, :][None] + came[:, part, :] * b[k : k + 1, :][None]
        )
    for p in range(NXY):
        out[p, TOPS : TOPS + RB, :] = level
        out[p, TOPS + RB : SENT, :] = level[0 : SENT - TOPS - RB, :]


def finish_noise_body(nblk, came, out):
    levels = came[:, TOPS : TOPS + RB, :]
    shares = jnp.exp(levels - joined(levels)[None])
    for k in range(RB):
        part = slice(k * OWN, (k + 1) * OWN)
        total = jnp.sum(came[:, part, :] * shares[:, k : k + 1, :], axis=0)
        out[:, k * BLOCK : (k + 1) * BLOCK] = jnp.where(k < nblk[0], total, 0.0)


def pair_body(place, got, stay, came, *outs):
    level = joined(got[...])
    a = jnp.exp(got[place[0]] - level)
    b = jnp.exp(got[neighbour(place[0])] - level)
    for q in range(NZ // 2):
        for k in range(CB):
            part = slice(k * CHUNK, (k + 1) * CHUNK)
            outs[q][part, :] = stay[q, part, :] * a[k : k + 1, :] + came[q, part, :] * b[k : k + 1, :]


def finish_data_body(dblk, *refs):
    came, out = refs[: NZ // 2], refs[NZ // 2]
    for k in range(CB):
        part = slice(k * CHUNK, (k + 1) * CHUNK)
        total = (came[0][part, :] + came[1][part, :]) + (came[2][part, :] + came[3][part, :])
        out[:, k * BLOCK : (k + 1) * BLOCK] = jnp.where(k < dblk[0], total, 0.0)


CORES = [(0, 1), (1, 0)]
PAIRS = [(i, i ^ 1) for i in range(NZ)]


def shifted(s):
    return [(i, (i + s) % NZ) for i in range(NZ)]


def over_dp(lse):
    came = lax.ppermute(lse, "c", CORES)
    top = jnp.maximum(lse, came)
    both = top + jnp.log(jnp.exp(lse - top) + jnp.exp(came - top))
    counts = lax.broadcasted_iota(jnp.int32, (LROWS, BLOCK), 0) == RB
    both = jnp.where(counts, lse + came, both)
    return lax.all_to_all(
        jnp.broadcast_to(both[None], (NXY, LROWS, BLOCK)), ("x", "y"), 0, 0, tiled=True
    )


def over_noise(pieces):
    return lax.all_to_all(pieces, "z", 0, 0, tiled=True)


def on_device(noise_points, data_points, noise_blocks, data_blocks):
    place = lax.axis_index("z").reshape(1)
    core = lax.axis_index("c").reshape(1)
    mine, place, core = lax.optimization_barrier((data_points.T, place, core))
    own = [mine, lax.ppermute(mine, "z", shifted(2)), None, lax.ppermute(mine, "z", shifted(6))]
    own[2] = lax.ppermute(own[3], "z", shifted(6))
    left = lax.ppermute(jnp.concatenate([mine, own[1]]), "z", shifted(1))
    right = lax.ppermute(jnp.concatenate([mine, own[3]]), "z", shifted(NZ - 1))
    high, low, turned_high, turned_low, squares = call(
        prepare_body,
        (
            shaped((2, ROWS, DIM // 2), BF16),
            shaped((2, ROWS, DIM // 2), BF16),
            pltpu.HBM((DIM, ROWS), BF16),
            pltpu.HBM((DIM, ROWS), BF16),
            shaped((ROWS, 1)),
        ),
        [SMEM] * 4 + [HBM],
        [
            pltpu.VMEM((ROWS, DIM), F32),
            pltpu.VMEM((DIM, ROWS), BF16),
            pltpu.VMEM((DIM, ROWS), BF16),
            pltpu.SemaphoreType.DMA((3, ROWS // 256)),
        ],
        limit=8,
        places=(VMEM, VMEM, HBM, HBM, VMEM),
    )(
        place,
        core,
        noise_blocks,
        data_blocks,
        pltpu.with_memory_space_constraint(noise_points, pltpu.HBM),
    )
    near = call(
        near_body,
        shaped((ROWS, COLS)),
        [SMEM] + [VMEM] * 7,
        [pltpu.VMEM((DIM // 2, COLS), BF16), pltpu.VMEM((DIM // 2, COLS), BF16)],
        limit=6,
    )(place, high, low, squares, *own)
    cost, lse, turned = call(
        cost_body,
        (shaped((ROWS, COLS)), shaped((LROWS, BLOCK)), shaped((NC, 2, DIM // NC, COLS), BF16)),
        [SMEM, SMEM] + [VMEM] * 9,
        [pltpu.VMEM((DIM // 2, COLS), BF16), pltpu.VMEM((DIM // 2, COLS), BF16)],
        limit=6,
    )(place, data_blocks, high, low, near, left, right, *own)
    for turn in range(ITERS):
        if turn:
            lse = call(row_body, shaped((LROWS, BLOCK)), [SMEM, VMEM, VMEM])(data_blocks, got, cost)
        rows = over_dp(lse)
        sent, dual = call(
            column_body,
            (shaped((NZ, 8, BLOCK)), shaped((LROWS, BLOCK))),
            [SMEM, VMEM, VMEM],
            [pltpu.VMEM((ROWS, 1), F32)],
        )(noise_blocks, rows, cost)
        got = over_noise(sent)
    stay, away = call(
        project_noise_body,
        [pltpu.HBM((NZ // 2, CB * CHUNK, BLOCK), F32) for _ in range(2)],
        [SMEM, SMEM, VMEM, VMEM, VMEM, HBM, HBM],
        [
            pltpu.VMEM((NZ, CB * CHUNK, BLOCK), F32),
            pltpu.VMEM((DIM, ROWS), BF16),
            pltpu.VMEM((DIM, ROWS), BF16),
            pltpu.VMEM((ROWS, COLS), BF16),
            pltpu.VMEM((ROWS, COLS), BF16),
            pltpu.SemaphoreType.DMA((2 + NZ,)),
        ],
        places=[HBM] * 2,
    )(
        place,
        noise_blocks,
        sent,
        dual,
        cost,
        pltpu.with_memory_space_constraint(turned_high, pltpu.HBM),
        pltpu.with_memory_space_constraint(turned_low, pltpu.HBM),
    )
    got, stay, away = lax.optimization_barrier((got, stay, away))
    paired = lax.ppermute(away, "z", PAIRS)
    summed = call(
        pair_body, [shaped((CB * CHUNK, BLOCK)) for _ in range(NZ // 2)], [SMEM, VMEM, VMEM, VMEM]
    )(
        place,
        got,
        pltpu.with_memory_space_constraint(stay, pltpu.HBM),
        pltpu.with_memory_space_constraint(paired, pltpu.HBM),
    )
    data_came = [summed[0]] + [
        lax.ppermute(summed[q], "z", shifted(2 * q)) for q in (1, 2, 3)
    ]
    theirs, weights_high, weights_low, data_dual, level = call(
        project_data_body,
        (
            shaped((NXY, PIECE, BLOCK)),
            shaped((ROWS, COLS), BF16),
            shaped((ROWS, COLS), BF16),
            shaped((1, COLS)),
            shaped((2 * RB, BLOCK)),
        ),
        [SMEM, SMEM, VMEM, VMEM, VMEM],
    )(core, data_blocks, got, cost, turned)
    came = lax.ppermute(theirs, "c", CORES)
    own = call(
        project_own_body, shaped((NXY, RB * OWN, BLOCK)), [SMEM, VMEM, VMEM, VMEM]
    )(core, turned, weights_high, weights_low)
    merged = call(merge_body, pltpu.VMEM((NXY, SENT, BLOCK), F32), [VMEM] * 3)(own, level, came)
    noise_came = lax.all_to_all(merged, ("x", "y"), 0, 0, tiled=True)
    noise_target = call(finish_noise_body, shaped((OWN, ROWS)), [SMEM, VMEM])(
        noise_blocks, noise_came
    )
    data_target = call(
        finish_data_body, shaped((CHUNK, COLS)), [SMEM] + [VMEM] * (NZ // 2)
    )(data_blocks, *data_came)
    row_live = jnp.arange(ROWS, dtype=jnp.int32) < noise_blocks[0] * BLOCK
    column_live = jnp.arange(COLS, dtype=jnp.int32) < data_blocks[0] * BLOCK
    noise_potential = jnp.where(row_live, SMOOTHING_TEMP * dual[:RB].reshape(ROWS), 0.0)
    data_potential = jnp.where(column_live, SMOOTHING_TEMP * data_dual.reshape(COLS), 0.0)
    return noise_potential, data_potential, noise_target, data_target


def solution(mesh):
    axes = Mesh(mesh.devices.reshape(NZ, 4, 4, NC), ("z", "x", "y", "c"))
    dp = ("x", "y", "c")
    return jax.shard_map(
        on_device,
        mesh=axes,
        in_specs=(P("z", None), P(dp, "z"), P("z"), P(dp)),
        out_specs=(P("z"), P(dp), P(dp, "z"), P("z", dp)),
        check_vma=False,
    )
```

```python
import jax
import jax.numpy as jnp
from jax import lax
from jax.experimental import pallas as pl
from jax.experimental.pallas import tpu as pltpu
from jax.sharding import Mesh, PartitionSpec as P


BLOCK = 128
ITERS = 3
SMOOTHING_TEMP = 0.125
SHARP = 1.0 / SMOOTHING_TEMP

F32 = jnp.float32
BF16 = jnp.bfloat16
NZ, NXY, NC = 8, 16, 2
ROWS, COLS, DIM = 1536, 384, 512
RB, CB = ROWS // BLOCK, COLS // BLOCK
CHUNK = DIM // NZ
OWN = DIM // (NXY * NC)
LROWS = 16
TOPS = RB * OWN
LEVELS = TOPS + RB
PIECE = TOPS + 2 * RB
SENT = TOPS + LROWS

SMEM = pl.BlockSpec(memory_space=pltpu.SMEM)
VMEM = pl.BlockSpec(memory_space=pltpu.VMEM)
HBM = pl.BlockSpec(memory_space=pltpu.HBM)


def shaped(shape, dtype=F32):
    return jax.ShapeDtypeStruct(shape, dtype)


def call(body, outs, ins, scratch=(), limit=16, places=None):
    return pl.pallas_call(
        body,
        out_shape=outs,
        in_specs=ins,
        out_specs=places or jax.tree.map(lambda _: VMEM, outs),
        scratch_shapes=scratch,
        cost_estimate=pl.CostEstimate(flops=1000000, transcendentals=0, bytes_accessed=4000000),
        compiler_params=pltpu.CompilerParams(vmem_limit_bytes=limit << 20),
    )


def halves(value):
    high = value.astype(BF16)
    return high, (value - high.astype(F32)).astype(BF16)


def dot(a, b, dims):
    return lax.dot_general(a, b, (dims, ((), ())), preferred_element_type=F32)


def dot3(a, b, dims):
    return dot(a[0], b[0], dims) + (dot(a[0], b[1], dims) + dot(a[1], b[0], dims))


def diagonal():
    return lax.broadcasted_iota(jnp.int32, (BLOCK, BLOCK), 0) == lax.broadcasted_iota(
        jnp.int32, (BLOCK, BLOCK), 1
    )


def to_row(column, eye):
    return jnp.sum(jnp.where(eye, column, 0.0), axis=0, keepdims=True)


def to_column(row, eye):
    return jnp.sum(jnp.where(eye, jnp.broadcast_to(row, (BLOCK, BLOCK)), 0.0), axis=1, keepdims=True)


PARTS = [slice(k, k + 256) for k in range(0, ROWS, 256)]


def loading(points, rows, sems):
    loads = [
        pltpu.make_async_copy(points.at[part, :], rows.at[part, :], sems.at[0, n])
        for n, part in enumerate(PARTS)
    ]
    for load in loads:
        load.start()
    return loads


def prepare_body(place, core, nblk, dblk, points, high, low, squares, rows, sems):
    loads = loading(points, rows, sems)
    for n, part in enumerate(PARTS):
        loads[n].wait()
        some = rows[part, :]
        squares[part, :] = jnp.sum(some * some, axis=1, keepdims=True)
        a, b = halves(some)
        for p in range(2):
            for q in range(NZ // 2):
                take = slice((2 * q + p) * CHUNK, (2 * q + p + 1) * CHUNK)
                high[p, part, q * CHUNK : (q + 1) * CHUNK] = a[:, take]
                low[p, part, q * CHUNK : (q + 1) * CHUNK] = b[:, take]


def flip_body(points, turned_high, turned_low, rows, th, tl, sems):
    loads = loading(points, rows, sems)
    stores = []
    for n, part in enumerate(PARTS):
        loads[n].wait()
        a, b = halves(rows[part, :].T)
        th[:, part] = a
        tl[:, part] = b
        for m, (source, out) in enumerate(((th, turned_high), (tl, turned_low))):
            store = pltpu.make_async_copy(source.at[:, part], out.at[:, part], sems.at[1 + m, n])
            store.start()
            stores.append(store)
    for store in stores:
        store.wait()


def row_lse(cost, bias, k):
    scores = bias - cost[k * BLOCK : (k + 1) * BLOCK, :]
    top = jnp.max(scores, axis=1, keepdims=True)
    return top + jnp.log(jnp.sum(jnp.exp(scores - top), axis=1, keepdims=True))


def live_columns(dblk):
    return lax.broadcasted_iota(jnp.int32, (1, COLS), 1) < dblk[0] * BLOCK


def store_count(out, row, count):
    out[row : row + 1, :] = jnp.full((1, BLOCK), (count * BLOCK).astype(F32))


def neighbour(z):
    return z + 1 - 2 * lax.rem(z, 2)


def near_pieces(z, refs):
    return [(lax.rem(z + (NZ - 2 * q), NZ), refs[q][...]) for q in range(NZ // 2)]


def far_pieces(z, refs):
    shifts = (NZ - 1, 1, NZ - 3, 3)
    return [(lax.rem(z + shift, NZ), ref[...]) for shift, ref in zip(shifts, refs)]


def half_product(side, pieces, high, low, data_high, data_low):
    square = jnp.zeros((1, COLS), F32)
    for source, piece in pieces:
        square += jnp.sum(piece * piece, axis=0, keepdims=True)
        a, b = halves(piece)
        at = pl.multiple_of(lax.div(source, 2) * CHUNK, CHUNK)
        data_high[pl.ds(at, CHUNK), :] = a
        data_low[pl.ds(at, CHUNK), :] = b
    both = (data_high[...], data_low[...])

    def cross(k):
        part = slice(k, k + 256)
        return square - 2.0 * dot3((high[side, part, :], low[side, part, :]), both, ((1,), (0,)))

    return cross


def turn(turned, pieces):
    for source, piece in pieces:
        for h in range(CHUNK // OWN):
            a, b = halves(piece[h * OWN : (h + 1) * OWN, :])
            to = pl.multiple_of((source * 2 + h // 2) * OWN, OWN)
            turned[h % 2, 0, pl.ds(to, OWN), :] = a
            turned[h % 2, 1, pl.ds(to, OWN), :] = b


def near_body(place, high, low, squares, *refs):
    pieces, (cost, data_high, data_low) = near_pieces(place[0], refs[:4]), refs[4:]
    cross = half_product(lax.rem(place[0], 2), pieces, high, low, data_high, data_low)
    for k in range(0, ROWS, 256):
        cost[k : k + 256, :] = squares[k : k + 256, :] + cross(k)


def cost_body(place, dblk, high, low, near, *refs):
    z, own, (cost, out, turned, data_high, data_low) = place[0], refs[:4], refs[8:]
    pieces = far_pieces(z, refs[4:8])
    cross = half_product(1 - lax.rem(z, 2), pieces, high, low, data_high, data_low)
    eye = diagonal()
    bias = jnp.where(live_columns(dblk), 0.0, -jnp.inf)
    out[...] = jnp.zeros((LROWS, BLOCK), F32)
    for k in range(0, ROWS, 256):
        cost[k : k + 256, :] = SHARP * (near[k : k + 256, :] + cross(k))
    for k in range(RB):
        out[k : k + 1, :] = to_row(row_lse(cost, bias, k), eye)
    store_count(out, RB, dblk[0])
    turn(turned, pieces + near_pieces(z, own))


def joined(values):
    top = jnp.max(values, axis=0)
    return top + jnp.log(jnp.sum(jnp.exp(values - top[None]), axis=0))


def column_bias(got, dblk):
    values = got[...]
    total = jnp.sum(values[:, CB, :], axis=0, keepdims=True)
    level = joined(values)
    parts = [-(level[k : k + 1, :] - jnp.log(total)) for k in range(CB)]
    return jnp.where(live_columns(dblk), jnp.concatenate(parts, axis=1), -jnp.inf)


def row_body(dblk, got, cost, out):
    bias = column_bias(got, dblk)
    eye = diagonal()
    out[...] = jnp.zeros((LROWS, BLOCK), F32)
    for k in range(RB):
        out[k : k + 1, :] = to_row(row_lse(cost, bias, k), eye)
    store_count(out, RB, dblk[0])


def column_body(nblk, got, cost, out, dual, column):
    values = got[...]
    total = jnp.sum(values[:, RB, :], axis=0, keepdims=True)
    duals = -(joined(values) - jnp.log(total))
    dual[...] = duals
    eye = diagonal()
    tops = []
    for k in range(RB):
        row = jnp.where(k < nblk[0], duals[k : k + 1, :], -jnp.inf)
        bias = to_column(row, eye)
        column[k * BLOCK : (k + 1) * BLOCK, :] = bias
        scores = bias - cost[k * BLOCK : (k + 1) * BLOCK, :]
        tops.append(jnp.max(scores.reshape(BLOCK // 8, 8, COLS), axis=0))
    top = tops[0]
    for k in range(1, RB):
        top = jnp.maximum(top, tops[k])
    top = jnp.max(top, axis=0, keepdims=True)
    mass = jnp.zeros((8, COLS), F32)
    for k in range(RB):
        part = slice(k * BLOCK, (k + 1) * BLOCK)
        scores = jnp.exp(column[part, :] - cost[part, :] - top)
        mass += jnp.sum(scores.reshape(BLOCK // 8, 8, COLS), axis=0)
    level = top + jnp.log(jnp.sum(mass, axis=0, keepdims=True))
    value = jnp.concatenate(
        [level[:, k * BLOCK : (k + 1) * BLOCK] for k in range(CB)]
        + [jnp.full((1, BLOCK), (nblk[0] * BLOCK).astype(F32))]
        + [jnp.zeros((8 - CB - 1, BLOCK), F32)],
        axis=0,
    )
    for z in range(NZ):
        out[z] = value


def project_noise_body(place, nblk, own, dual, cost, turned_high, turned_low, *refs):
    stay, away, whole, th, tl, weights_high, weights_low, sems = refs
    copies = [
        pltpu.make_async_copy(turned_high, th, sems.at[0]),
        pltpu.make_async_copy(turned_low, tl, sems.at[1]),
    ]
    for copy in copies:
        copy.start()
    level = jnp.concatenate([own[0, k : k + 1, :] for k in range(CB)], axis=1)
    eye = diagonal()
    for k in range(RB):
        part = slice(k * BLOCK, (k + 1) * BLOCK)
        row = jnp.where(k < nblk[0], dual[k : k + 1, :], -jnp.inf)
        a, b = halves(jnp.exp(to_column(row, eye) - cost[part, :] - level))
        weights_high[part, :] = a
        weights_low[part, :] = b
    for copy in copies:
        copy.wait()
    both = (weights_high[...], weights_low[...])
    for k in range(0, DIM, 256):
        some = dot3((th[k : k + 256, :], tl[k : k + 256, :]), both, ((1,), (0,)))
        for q in range(256 // CHUNK):
            for c in range(CB):
                whole[k // CHUNK + q, c * CHUNK : (c + 1) * CHUNK, :] = some[
                    q * CHUNK : (q + 1) * CHUNK, c * BLOCK : (c + 1) * BLOCK
                ]
    z = place[0]
    moves = []
    for q in range(NZ // 2):
        for n, (source, out) in enumerate(((neighbour(z), away), (z, stay))):
            take = whole.at[lax.rem(source + 2 * q, NZ)]
            moves.append(pltpu.make_async_copy(take, out.at[q], sems.at[2 + 2 * q + n]))
    for move in moves:
        move.start()
    for move in moves:
        move.wait()


def spread(out, some, k):
    for p in range(NXY):
        for h in range(2):
            out[p, (k * 2 + h) * OWN : (k * 2 + h + 1) * OWN, :] = some[
                p * OWN : (p + 1) * OWN, h * BLOCK : (h + 1) * BLOCK
            ]


def project_data_body(core, dblk, got, cost, turned, out, high, low, dual, tops):
    bias = column_bias(got, dblk)
    dual[...] = bias
    eye = diagonal()
    for k in range(RB):
        part = slice(k * BLOCK, (k + 1) * BLOCK)
        scores = bias - cost[part, :]
        top = jnp.max(scores, axis=1, keepdims=True)
        weights = jnp.exp(scores - top)
        level = top + jnp.log(jnp.sum(weights, axis=1, keepdims=True))
        tops[k : k + 1, :] = to_row(top, eye)
        tops[RB + k : RB + k + 1, :] = to_row(level, eye)
        a, b = halves(weights)
        high[part, :] = a
        low[part, :] = b
    other = 1 - core[0]
    for k in range(ROWS // 256):
        part = slice(k * 256, (k + 1) * 256)
        some = dot3((turned[other, 0], turned[other, 1]), (high[part, :], low[part, :]), ((1,), (1,)))
        spread(out, some, k)
    for p in range(NXY):
        out[p, TOPS:PIECE, :] = tops[...]


def project_own_body(core, turned, high, low, out):
    mine = core[0]
    for k in range(ROWS // 256):
        part = slice(k * 256, (k + 1) * 256)
        some = dot3((turned[mine, 0], turned[mine, 1]), (high[part, :], low[part, :]), ((1,), (1,)))
        spread(out, some, k)


def merge_body(own, own_tops, came, out):
    a, b = own_tops[RB : 2 * RB, :], came[0, LEVELS:PIECE, :]
    top = jnp.maximum(a, b)
    level = top + jnp.log(jnp.exp(a - top) + jnp.exp(b - top))
    a, b = jnp.exp(own_tops[0:RB, :] - level), jnp.exp(came[0, TOPS:LEVELS, :] - level)
    for k in range(RB):
        part = slice(k * OWN, (k + 1) * OWN)
        out[:, part, :] = (
            own[:, part, :] * a[k : k + 1, :][None] + came[:, part, :] * b[k : k + 1, :][None]
        )
    for p in range(NXY):
        out[p, TOPS : TOPS + RB, :] = level
        out[p, TOPS + RB : SENT, :] = level[0 : SENT - TOPS - RB, :]


def finish_noise_body(nblk, came, out):
    levels = came[:, TOPS : TOPS + RB, :]
    shares = jnp.exp(levels - joined(levels)[None])
    for k in range(RB):
        part = slice(k * OWN, (k + 1) * OWN)
        total = jnp.sum(came[:, part, :] * shares[:, k : k + 1, :], axis=0)
        out[:, k * BLOCK : (k + 1) * BLOCK] = jnp.where(k < nblk[0], total, 0.0)


def pair_body(place, got, stay, came, *outs):
    level = joined(got[...])
    a = jnp.exp(got[place[0]] - level)
    b = jnp.exp(got[neighbour(place[0])] - level)
    for q in range(NZ // 2):
        for k in range(CB):
            part = slice(k * CHUNK, (k + 1) * CHUNK)
            outs[q][part, :] = stay[q, part, :] * a[k : k + 1, :] + came[q, part, :] * b[k : k + 1, :]


def finish_data_body(dblk, *refs):
    came, out = refs[: NZ // 2], refs[NZ // 2]
    for k in range(CB):
        part = slice(k * CHUNK, (k + 1) * CHUNK)
        total = (came[0][part, :] + came[1][part, :]) + (came[2][part, :] + came[3][part, :])
        out[:, k * BLOCK : (k + 1) * BLOCK] = jnp.where(k < dblk[0], total, 0.0)


CORES = [(0, 1), (1, 0)]
PAIRS = [(i, i ^ 1) for i in range(NZ)]


def shifted(s):
    return [(i, (i + s) % NZ) for i in range(NZ)]


def over_dp(lse):
    came = lax.ppermute(lse, "c", CORES)
    top = jnp.maximum(lse, came)
    both = top + jnp.log(jnp.exp(lse - top) + jnp.exp(came - top))
    counts = lax.broadcasted_iota(jnp.int32, (LROWS, BLOCK), 0) == RB
    both = jnp.where(counts, lse + came, both)
    return lax.all_to_all(
        jnp.broadcast_to(both[None], (NXY, LROWS, BLOCK)), ("x", "y"), 0, 0, tiled=True
    )


def over_noise(pieces):
    return lax.all_to_all(pieces, "z", 0, 0, tiled=True)


def on_device(noise_points, data_points, noise_blocks, data_blocks):
    place = lax.axis_index("z").reshape(1)
    core = lax.axis_index("c").reshape(1)
    mine, place, core = lax.optimization_barrier((data_points.T, place, core))
    own = [mine, lax.ppermute(mine, "z", shifted(2)), None, lax.ppermute(mine, "z", shifted(6))]
    odd = [lax.ppermute(mine, "z", shifted(1)), lax.ppermute(mine, "z", shifted(NZ - 1))]
    odd.append(lax.ppermute(own[1], "z", shifted(1)))
    odd.append(lax.ppermute(own[3], "z", shifted(NZ - 1)))
    own[2] = lax.ppermute(own[3], "z", shifted(6))
    points = pltpu.with_memory_space_constraint(noise_points, pltpu.HBM)
    high, low, squares = call(
        prepare_body,
        (
            shaped((2, ROWS, DIM // 2), BF16),
            shaped((2, ROWS, DIM // 2), BF16),
            shaped((ROWS, 1)),
        ),
        [SMEM] * 4 + [HBM],
        [pltpu.VMEM((ROWS, DIM), F32), pltpu.SemaphoreType.DMA((1, ROWS // 256))],
        limit=8,
    )(place, core, noise_blocks, data_blocks, points)
    turned_high, turned_low = call(
        flip_body,
        (pltpu.HBM((DIM, ROWS), BF16), pltpu.HBM((DIM, ROWS), BF16)),
        [HBM],
        [
            pltpu.VMEM((ROWS, DIM), F32),
            pltpu.VMEM((DIM, ROWS), BF16),
            pltpu.VMEM((DIM, ROWS), BF16),
            pltpu.SemaphoreType.DMA((3, ROWS // 256)),
        ],
        limit=8,
        places=(HBM, HBM),
    )(points)
    near = call(
        near_body,
        shaped((ROWS, COLS)),
        [SMEM] + [VMEM] * 7,
        [pltpu.VMEM((DIM // 2, COLS), BF16), pltpu.VMEM((DIM // 2, COLS), BF16)],
        limit=6,
    )(place, high, low, squares, *own)
    cost, lse, turned = call(
        cost_body,
        (shaped((ROWS, COLS)), shaped((LROWS, BLOCK)), shaped((NC, 2, DIM // NC, COLS), BF16)),
        [SMEM, SMEM] + [VMEM] * 11,
        [pltpu.VMEM((DIM // 2, COLS), BF16), pltpu.VMEM((DIM // 2, COLS), BF16)],
        limit=6,
    )(place, data_blocks, high, low, near, *own, *odd)
    for turn in range(ITERS):
        if turn:
            lse = call(row_body, shaped((LROWS, BLOCK)), [SMEM, VMEM, VMEM])(data_blocks, got, cost)
        rows = over_dp(lse)
        sent, dual = call(
            column_body,
            (shaped((NZ, 8, BLOCK)), shaped((LROWS, BLOCK))),
            [SMEM, VMEM, VMEM],
            [pltpu.VMEM((ROWS, 1), F32)],
        )(noise_blocks, rows, cost)
        got = over_noise(sent)
    stay, away = call(
        project_noise_body,
        [pltpu.HBM((NZ // 2, CB * CHUNK, BLOCK), F32) for _ in range(2)],
        [SMEM, SMEM, VMEM, VMEM, VMEM, HBM, HBM],
        [
            pltpu.VMEM((NZ, CB * CHUNK, BLOCK), F32),
            pltpu.VMEM((DIM, ROWS), BF16),
            pltpu.VMEM((DIM, ROWS), BF16),
            pltpu.VMEM((ROWS, COLS), BF16),
            pltpu.VMEM((ROWS, COLS), BF16),
            pltpu.SemaphoreType.DMA((2 + NZ,)),
        ],
        places=[HBM] * 2,
    )(
        place,
        noise_blocks,
        sent,
        dual,
        cost,
        pltpu.with_memory_space_constraint(turned_high, pltpu.HBM),
        pltpu.with_memory_space_constraint(turned_low, pltpu.HBM),
    )
    got, stay, away = lax.optimization_barrier((got, stay, away))
    paired = lax.ppermute(away, "z", PAIRS)
    summed = call(
        pair_body, [shaped((CB * CHUNK, BLOCK)) for _ in range(NZ // 2)], [SMEM, VMEM, VMEM, VMEM]
    )(
        place,
        got,
        stay,
        paired,
    )
    data_came = [summed[0]] + [
        lax.ppermute(summed[q], "z", shifted(2 * q)) for q in (1, 2, 3)
    ]
    theirs, weights_high, weights_low, data_dual, level = call(
        project_data_body,
        (
            shaped((NXY, PIECE, BLOCK)),
            shaped((ROWS, COLS), BF16),
            shaped((ROWS, COLS), BF16),
            shaped((1, COLS)),
            shaped((2 * RB, BLOCK)),
        ),
        [SMEM, SMEM, VMEM, VMEM, VMEM],
    )(core, data_blocks, got, cost, turned)
    came = lax.ppermute(theirs, "c", CORES)
    own = call(
        project_own_body, shaped((NXY, RB * OWN, BLOCK)), [SMEM, VMEM, VMEM, VMEM]
    )(core, turned, weights_high, weights_low)
    merged = call(merge_body, pltpu.VMEM((NXY, SENT, BLOCK), F32), [VMEM] * 3)(own, level, came)
    noise_came = lax.all_to_all(merged, ("x", "y"), 0, 0, tiled=True)
    noise_target = call(finish_noise_body, shaped((OWN, ROWS)), [SMEM, VMEM])(
        noise_blocks, noise_came
    )
    data_target = call(
        finish_data_body, shaped((CHUNK, COLS)), [SMEM] + [VMEM] * (NZ // 2)
    )(data_blocks, *data_came)
    row_live = jnp.arange(ROWS, dtype=jnp.int32) < noise_blocks[0] * BLOCK
    column_live = jnp.arange(COLS, dtype=jnp.int32) < data_blocks[0] * BLOCK
    noise_potential = jnp.where(row_live, SMOOTHING_TEMP * dual[:RB].reshape(ROWS), 0.0)
    data_potential = jnp.where(column_live, SMOOTHING_TEMP * data_dual.reshape(COLS), 0.0)
    return noise_potential, data_potential, noise_target, data_target


def solution(mesh):
    axes = Mesh(mesh.devices.reshape(NZ, 4, 4, NC), ("z", "x", "y", "c"))
    dp = ("x", "y", "c")
    return jax.shard_map(
        on_device,
        mesh=axes,
        in_specs=(P("z", None), P(dp, "z"), P("z"), P(dp)),
        out_specs=(P("z"), P(dp), P(dp, "z"), P("z", dp)),
        check_vma=False,
    )
```
